512 devices in a mesh: tm: 32 (over z, y_lo, core), depth: 16 (over x, y_hi).
Axes of the slice: x: 4, y: 8 (y_hi: 4, y_lo: 2; y = y_hi * 2 + y_lo), z: 8, core: 2. Of those that a mesh axis runs over, the one named last changes fastest.
Arguments:
- raw: bfloat16 [512, 128, 128], P('tm', 'depth'), may hold values from -6 to 6
- stream: bfloat16 [512, 128, 2048], P('tm', 'depth'), may hold values from -6 to 6
- conv_w: bfloat16 [3, 128, 2048], replicated, may hold values from -0.3125 to 0.3125
- gain: float32 [2048], replicated, may hold values from 0.1 to 1.9
- w_qkv: bfloat16 [2048, 3072], P('tm', 'depth'), may hold values from -4 to 4
- mask: int32 [16, 32, 5], P('depth', 'tm'), may hold values from 0 to 1, as said below
Outputs:
- context: bfloat16 [512, 128, 1024], P('tm', 'depth')
The draws below stay inside these ranges and needn't reach their ends.
Inputs may be any that keep to these rules, and one draw needn't show every extreme that they name: mask[p, i, 2] = 1 for every block; mask[p, i, e] = 0 wherever i + e - 2 lies outside 0 to 31.
All inputs are finite; a program needn't handle non-finite values.
Results may differ from the reference program's by a relative error of at most 0.012.
The reference program's roundings to bfloat16 on the way (of `normed`, `projected` and `weights`) count: a program that leaves them out, or rounds other values in their place, can miss the bound.
Values may be sent and summed in bfloat16 or wider, within the bound.
A program may use at most 64 MiB of HBM per device.

```python
import math
import jax
import jax.numpy as jnp
from jax import lax

D = 2048
HEADS = 8
HD = 128
F_IN = 128
BT = 16
PP = 8
NT = 512
NP = 128
NTB = 32
RB = 2
KSPAN = 5
N_DEPTH = 16


def draw_w_qkv(key, part):
    head_cols = HEADS * HD
    first_key = jax.random.fold_in(jax.random.fold_in(key, 11), 0)
    scales = jnp.concatenate([jnp.full((2 * head_cols,), 2.0, jnp.float32), jnp.ones((head_cols,), jnp.float32)]) / math.sqrt(D)
    matrix = jax.random.normal(first_key, (D, 3 * head_cols), jnp.float32) * scales
    return jnp.clip(matrix, -4.0, 4.0).astype(jnp.bfloat16)


def draw_mask(key, part):
    level_key, coin_key = jax.random.split(jax.random.fold_in(key, 5))
    levels = jax.random.randint(level_key, (N_DEPTH, NTB, 1), 0, 5)
    coin_draws = jax.random.randint(coin_key, (N_DEPTH, NTB, KSPAN), 0, 4)
    offsets = jnp.arange(KSPAN, dtype=jnp.int32)[None, None, :] - RB
    blocks = jnp.arange(NTB, dtype=jnp.int32)[None, :, None] + offsets
    inside = (blocks >= 0) & (blocks < NTB)
    chosen = (coin_draws < levels) | (offsets == 0)
    return jnp.where(inside & chosen, 1, 0).astype(jnp.int32)


def block_scale(key, extent, pieces, low, largest):
    factor_of, own = 1.0, jax.random.fold_in(key, 6)
    for dim, parts in pieces:
        draws = jnp.exp(jax.random.uniform(jax.random.fold_in(own, dim), (parts,), jnp.float32, low / len(pieces), largest / len(pieces)))
        factor_of = factor_of * jnp.repeat(draws, extent[dim] // parts).reshape([-1 if axis == dim else 1 for axis in range(len(extent))])
    return factor_of


def noise(own_key, extent, width, limit, shards=(), kind=jnp.bfloat16):
    loudness = block_scale(own_key, extent, shards, -0.22, 0.18) if shards else 1.0
    values = jax.random.normal(own_key, extent, jnp.float32) * width * loudness
    return jnp.minimum(jnp.maximum(values, -limit), limit).astype(kind)


def setup_inputs(seed: int = 0) -> dict:
    seeds = jax.random.split(jax.random.key(seed), 7)
    return {
        "raw": noise(seeds[0], (NT, NP, F_IN), 1.0, 6.0, ((0, 32), (1, 16))),
        "stream": noise(seeds[1], (NT, NP, D), 1.0, 6.0, ((0, 32), (1, 16))),
        "conv_w": noise(seeds[2], (3, F_IN, D), (3 * F_IN) ** -0.5, 0.3125),
        "gain": jnp.clip(1.0 + 0.18 * jax.random.normal(seeds[3], (D,), jnp.float32), 0.1, 1.9),
        "w_qkv": draw_w_qkv(jax.random.fold_in(seeds[6], 71), 0),
        "mask": draw_mask(jax.random.fold_in(seeds[6], 71), 0),
    }


def attend(query_block, key_rows, value_rows, allowed):
    inv_root = 1.0 / math.sqrt(HD)
    scores = jnp.einsum('qhd,khd->hqk', query_block.astype(jnp.float32), key_rows.astype(jnp.float32)) * inv_root
    scores = jnp.where(allowed[None, None, :], scores, -1e+30)
    row_max = lax.optimization_barrier(jnp.max(scores, axis=-1, keepdims=True))
    powers = jnp.exp(scores - row_max)
    weights = (powers / lax.optimization_barrier(jnp.sum(powers, axis=-1, keepdims=True))).astype(jnp.bfloat16)
    result = jnp.einsum('hqk,khd->qhd', weights.astype(jnp.float32), value_rows.astype(jnp.float32))
    return result.reshape(query_block.shape[0], HEADS * HD).astype(jnp.bfloat16)

def reference(raw, stream, conv_w, gain, w_qkv, mask):
    tokens_all = NT * NP
    padded = jnp.pad(raw, ((0, 0), (1, 1), (0, 0)))
    embedded = stream.reshape(tokens_all, D).astype(jnp.float32)
    for offset in range(3):
        window = padded[:, offset:offset + NP].reshape(tokens_all, F_IN)
        embedded = embedded + jnp.dot(window, conv_w[offset], preferred_element_type=jnp.float32)
    normed = (embedded * lax.rsqrt(lax.optimization_barrier(jnp.mean(embedded * embedded, axis=-1, keepdims=True)) + 1e-05) * gain).astype(jnp.bfloat16)
    projected = jnp.dot(normed, w_qkv, preferred_element_type=jnp.float32).astype(jnp.bfloat16)
    block_rows = BT * PP
    head_cols = HEADS * HD
    width_all = 3 * head_cols
    blocked = projected.reshape(NTB, BT, N_DEPTH, PP, width_all).transpose(2, 0, 1, 3, 4).reshape(N_DEPTH, NTB, block_rows, width_all)
    queries = blocked[..., :head_cols]
    keyvals = jnp.pad(blocked[..., head_cols:], ((0, 0), (RB, RB), (0, 0), (0, 0)))
    mask_int = mask.astype(jnp.int32)

    def one_block(index):
        index = index.astype(jnp.int32)
        zero = jnp.zeros((), jnp.int32)
        depth_index = (index // NTB).astype(jnp.int32)
        time_index = (index % NTB).astype(jnp.int32)
        query_block = lax.dynamic_slice(queries, (depth_index, time_index, zero, zero), (1, 1, block_rows, head_cols)).reshape(block_rows, HEADS, HD)
        neighbourhood = lax.dynamic_slice(keyvals, (depth_index, time_index, zero, zero), (1, KSPAN, block_rows, 2 * head_cols)).reshape(KSPAN * block_rows, 2 * head_cols)
        key_rows = neighbourhood[:, :head_cols].reshape(KSPAN * block_rows, HEADS, HD)
        value_rows = neighbourhood[:, head_cols:].reshape(KSPAN * block_rows, HEADS, HD)
        row_mask = lax.dynamic_slice(mask_int, (depth_index, time_index, zero), (1, 1, KSPAN)).reshape(KSPAN)
        allowed = jnp.repeat(row_mask, block_rows) > 0
        return attend(query_block, key_rows, value_rows, allowed)
    results = lax.map(one_block, jnp.arange(N_DEPTH * NTB, dtype=jnp.int32))
    return results.reshape(N_DEPTH, NTB, BT, PP, head_cols).transpose(1, 2, 0, 3, 4).reshape(NT, NP, head_cols)
```

```python
import math

import jax
import jax.numpy as jnp
from jax import lax
from jax.experimental import pallas as pl
from jax.experimental.pallas import tpu as pltpu
from jax.sharding import PartitionSpec as P

HEADS = 8
HD = 128
BF = jnp.bfloat16
F32 = jnp.float32


def layer(raw, stream, conv, gain, w, mrow, out, pad, rleft, rright, emb, tok, wy, wp, wfull, acc,
          q, kv, masks, ctx_out, ctx_in, s_w, r_w, s_raw, r_raw, s_m, r_m, s_d, r_d, s_t, r_t,
          s_z, r_z, s_kv, r_kv, s_c, r_c):
    tm, depth = lax.axis_index("tm"), lax.axis_index("depth")
    z, g = tm // 4, tm % 4
    x, yh = depth // 4, depth % 4
    up, down = (depth + 1) % 16, (depth + 15) % 16
    zr, zl = (z + 1) % 8, (z + 7) % 8

    def send(src, dst, s, r, to):
        return pltpu.make_async_remote_copy(
            src_ref=src, dst_ref=dst, send_sem=s, recv_sem=r, device_id=to,
            device_id_type=pl.DeviceIdType.MESH)

    barrier = pltpu.get_barrier_semaphore()

    def greet(a, b):
        pl.semaphore_signal(barrier, inc=1, device_id=(a, b), device_id_type=pl.DeviceIdType.MESH)

    for k in range(1, 4):
        greet(tm, 4 * x + (yh + k) % 4)
    greet(tm, up)
    greet(tm, down)
    greet(4 * zr + g, depth)
    greet(4 * zl + g, depth)
    for a in range(4):
        for b in range(4):
            if a or b:
                greet(4 * z + (g + a) % 4, 4 * ((x + b) % 4) + yh)
    pl.semaphore_wait(barrier, 22)

    w_copies = [send(w, wy.at[yh], s_w.at[k - 1], r_w.at[k - 1], (tm, 4 * x + (yh + k) % 4))
                for k in range(1, 4)]
    for c in w_copies:
        c.start()
    raw_up = send(raw, rleft, s_raw.at[0], r_raw.at[0], (tm, up))
    raw_down = send(raw, rright, s_raw.at[1], r_raw.at[1], (tm, down))
    raw_up.start()
    raw_down.start()
    m_copies = [send(mrow, masks.at[g], s_m.at[k - 1], r_m.at[k - 1], (4 * z + (g + k) % 4, depth))
                for k in range(1, 4)]
    for c in m_copies:
        c.start()
    masks[g] = mrow[...]
    wy[yh] = w[...]

    for c in w_copies:
        c.wait()
    parts = [wy[i].astype(F32) for i in range(4)]
    wp[0] = jnp.concatenate([parts[0], parts[1][:, :64]], axis=1).astype(BF)
    wp[1] = jnp.concatenate([parts[1][:, 64:], parts[2][:, :128]], axis=1).astype(BF)
    wp[2] = jnp.concatenate([parts[2][:, 128:], parts[3]], axis=1).astype(BF)
    rows = pl.ds(pl.multiple_of(g * 64, 64), 64)

    def direct(j, k):
        pair = 3 * x + j
        return send(wp.at[j], wfull.at[z, pair // 4, rows], s_d.at[j, k], r_d.at[pair // 4, g],
                    (4 * z + pair % 4, 4 * ((x + k) % 4) + yh))

    def kept(j):
        pair = 3 * x + j
        return pltpu.make_async_copy(wp.at[j], wfull.at[z, pair // 4, rows], r_d.at[pair // 4, g])

    for j in range(3):
        for k in range(1, 4):
            direct(j, k).start()

        @pl.when((3 * x + j) % 4 != g)
        def _():
            direct(j, 0).start()

        @pl.when((3 * x + j) % 4 == g)
        def _():
            kept(j).start()

    raw_up.wait()
    raw_down.wait()
    pad[:, 1:9, :] = raw[...].astype(F32)
    pad[:, 0:1, :] = jnp.where(depth == 0, 0.0, rleft[:, 7:8, :].astype(F32))
    pad[:, 9:10, :] = jnp.where(depth == 15, 0.0, rright[:, 0:1, :].astype(F32))
    windows = [pad[:, j:j + 8, :].reshape(128, 128).astype(BF) for j in range(3)]
    squares = jnp.zeros((128, 1), F32)
    for n in range(4):
        cols = slice(512 * n, 512 * n + 512)
        e = stream[:, cols].astype(F32)
        for j in range(3):
            e = e + jnp.dot(windows[j], conv[j, :, cols], preferred_element_type=F32)
        emb[:, cols] = e
        squares = squares + jnp.sum(e * e, axis=-1, keepdims=True)
    inv = lax.rsqrt(squares * (1.0 / 2048) + 1e-05)
    tok[g] = (emb[...] * inv * gain[...]).astype(BF)
    partner = g + 1 - 2 * (g % 2)
    across = (g + 2) % 4
    t_across = send(tok.at[g], tok.at[g], s_t.at[0], r_t.at[0], (4 * z + across, depth))
    t_partner = send(tok.at[g], tok.at[g], s_t.at[1], r_t.at[1], (4 * z + partner, depth))
    t_relay = send(tok.at[across], tok.at[across], s_t.at[2], r_t.at[2], (4 * z + partner, depth))
    t_across.start()
    t_partner.start()

    for kind in range(3):
        for i in range(4):
            pltpu.make_async_copy(wp.at[0], wfull.at[z, kind, pl.ds(64 * i, 64)], r_d.at[kind, i]).wait()

    def half(c, h):
        return wfull.at[c, :, pl.ds(128 * h, 128)]

    def ring(way, step, h):
        c = (z + 8 - step) % 8 if way == 0 else (z + step) % 8
        i = 2 * step + (h if step < 3 else 0)
        return send(half(c, h), half(c, h), s_z.at[way, i], r_z.at[way, i],
                    (4 * (zr if way == 0 else zl) + g, depth))

    def halves(way, step):
        return (0, 1) if step < 3 else (way,)

    def multiply(c, first):
        cols = pl.ds(pl.multiple_of(c * 256, 256), 256)

        def one(kind, carry):
            product = jnp.dot(tok[:, :, cols].reshape(512, 256), wfull[c, kind],
                              preferred_element_type=F32)
            acc[kind] = product if first else acc[kind] + product
            return carry

        lax.fori_loop(0, 3, one, 0)

    for h in (0, 1):
        for way in (0, 1):
            ring(way, 0, h).start()
    t_across.wait_recv()
    t_relay.start()
    t_partner.wait_recv()
    t_relay.wait_recv()
    multiply(z, True)
    for step in range(4):
        for h in (0, 1):
            for way in (0, 1):
                if h in halves(way, step):
                    ring(way, step, h).wait_recv()
                    if step < 3 and h in halves(way, step + 1):
                        ring(way, step + 1, h).start()
        multiply((z + 7 - step) % 8, False)
        if step < 3:
            multiply((z + 1 + step) % 8, False)

    for b in range(4):
        kv[2 + b, :, :256] = acc[1, 128 * b:128 * b + 128].astype(BF)
        kv[2 + b, :, 256:] = acc[2, 128 * b:128 * b + 128].astype(BF)
    kv_ahead = send(kv.at[pl.ds(4, 2)], kv.at[pl.ds(0, 2)], s_kv.at[0], r_kv.at[0], (4 * zr + g, depth))
    kv_back = send(kv.at[pl.ds(2, 2)], kv.at[pl.ds(6, 2)], s_kv.at[1], r_kv.at[1], (4 * zl + g, depth))
    kv_ahead.start()
    kv_back.start()
    for b in range(4):
        q[b] = acc[0, 128 * b:128 * b + 128].astype(BF)
    for c in m_copies:
        c.wait()
    kv_ahead.wait()
    kv_back.wait()

    def attend(b):
        allowed = masks[b][0:1, :] > 0.5
        halves_out = []
        for h in range(2):
            keys = kv[pl.ds(b, 5), :, 128 * h:128 * h + 128].reshape(640, 128)
            values = kv[pl.ds(b, 5), :, 256 + 128 * h:384 + 128 * h].reshape(640, 128)
            query = q[b, :, 128 * h:128 * h + 128]
            scores = lax.dot_general(query, keys, (((1,), (1,)), ((), ())),
                                     preferred_element_type=F32) * (1.0 / math.sqrt(HD))
            scores = jnp.where(allowed, scores, -1e30)
            powers = jnp.exp(scores - jnp.max(scores, axis=-1, keepdims=True))
            weights = (powers / jnp.sum(powers, axis=-1, keepdims=True)).astype(BF)
            halves_out.append(jnp.dot(weights, values, preferred_element_type=F32).astype(BF))
        return halves_out

    def give(k):
        return send(ctx_out.at[k - 1], ctx_in.at[g], s_c.at[k - 1], r_c.at[k - 1],
                    (4 * z + (g + k) % 4, depth))

    for k in (2, 3, 1, 0):
        pieces = attend((g + k) % 4)
        for h in range(2):
            if k:
                ctx_out[k - 1, :, 128 * h:128 * h + 128] = pieces[h]
            else:
                ctx_in[g, :, 128 * h:128 * h + 128] = pieces[h]
        if k:
            give(k).start()

    for j in range(3):
        for k in range(1, 4):
            direct(j, k).wait_send()

        @pl.when((3 * x + j) % 4 != g)
        def _():
            direct(j, 0).wait_send()

    t_across.wait_send()
    t_partner.wait_send()
    t_relay.wait_send()
    for way in (0, 1):
        for step in range(4):
            for h in halves(way, step):
                ring(way, step, h).wait_send()
    for k in (2, 3, 1):
        give(k).wait()
    for i in range(4):
        out[:, 256 * i:256 * i + 256] = ctx_in[i]


def per_device(raw, stream, conv_w, gain, w_qkv, mask):
    mrow = jnp.broadcast_to(jnp.repeat(mask.reshape(1, 5).astype(F32), 128, axis=1), (8, 640))
    vmem = pltpu.VMEM
    dma = pltpu.SemaphoreType.DMA
    context = pl.pallas_call(
        layer,
        out_shape=jax.ShapeDtypeStruct((128, 1024), BF),
        in_specs=[pl.BlockSpec(memory_space=pltpu.VMEM)] * 6,
        out_specs=pl.BlockSpec(memory_space=pltpu.VMEM),
        scratch_shapes=[
            vmem((16, 16, 128), F32), vmem((16, 8, 128), BF), vmem((16, 8, 128), BF),
            vmem((128, 2048), F32), vmem((4, 128, 2048), BF), vmem((4, 64, 192), BF),
            vmem((3, 64, 256), BF), vmem((8, 3, 256, 256), BF), vmem((3, 512, 256), F32),
            vmem((4, 128, 256), BF), vmem((8, 128, 512), BF), vmem((4, 8, 640), F32),
            vmem((3, 128, 256), BF), vmem((4, 128, 256), BF),
            dma((3,)), dma((3,)), dma((2,)), dma((2,)), dma((3,)), dma((3,)),
            dma((3, 4)), dma((3, 4)), dma((3,)), dma((3,)), dma((2, 7)), dma((2, 7)),
            dma((2,)), dma((2,)), dma((3,)), dma((3,)),
        ],
        compiler_params=pltpu.CompilerParams(
            collective_id=0, has_side_effects=True, vmem_limit_bytes=48 * 1024 * 1024),
    )(raw, stream.reshape(128, 2048), conv_w, gain.reshape(1, 2048), w_qkv, mrow)
    return context.reshape(16, 8, 1024)


def solution(mesh):
    in_specs = (P("tm", "depth", None), P("tm", "depth", None), P(), P(), P("tm", "depth"),
                P("depth", "tm", None))
    return jax.shard_map(per_device, mesh=mesh, in_specs=in_specs,
                         out_specs=P("tm", "depth", None), check_vma=False)
```

```python
import math

import jax
import jax.numpy as jnp
from jax import lax
from jax.experimental import pallas as pl
from jax.experimental.pallas import tpu as pltpu
from jax.sharding import PartitionSpec as P

HEADS = 8
HD = 128
BF = jnp.bfloat16
F32 = jnp.float32


def layer(raw_h, stream_h, conv_h, gain_h, w_h, mrow, out, raw, stream, conv, gain, pad, rleft, rright,
          emb, tok, wy, wp, wfull, acc, q, kv, masks, ctx_out, ctx_in, s_in, s_w, r_w, s_raw, r_raw,
          s_m, r_m, s_d, r_d, s_e, r_e, s_t, r_t, s_z, r_z, s_b, r_b, s_x, r_x, s_f, r_f, s_kv, r_kv,
          s_c, r_c):
    tm, depth = lax.axis_index("tm"), lax.axis_index("depth")
    z, g = tm // 4, tm % 4
    x, yh = depth // 4, depth % 4
    up, down = (depth + 1) % 16, (depth + 15) % 16
    zr, zl = (z + 1) % 8, (z + 7) % 8
    xr, xl = (x + 1) % 4, (x + 3) % 4

    loads = [pltpu.make_async_copy(a, b, s_in.at[i]) for i, (a, b) in enumerate(
        ((w_h, wy.at[yh]), (raw_h, raw), (conv_h, conv), (stream_h, stream), (gain_h, gain)))]
    for c in loads:
        c.start()

    def send(src, dst, s, r, to):
        return pltpu.make_async_remote_copy(
            src_ref=src, dst_ref=dst, send_sem=s, recv_sem=r, device_id=to,
            device_id_type=pl.DeviceIdType.MESH)

    barrier = pltpu.get_barrier_semaphore()

    def greet(a, b):
        pl.semaphore_signal(barrier, inc=1, device_id=(a, b), device_id_type=pl.DeviceIdType.MESH)

    for k in range(1, 4):
        greet(tm, 4 * x + (yh + k) % 4)
    greet(tm, up)
    greet(tm, down)
    greet(4 * zr + g, depth)
    greet(4 * zl + g, depth)
    for a in range(4):
        for b in range(4):
            if a or b:
                greet(4 * z + (g + a) % 4, 4 * ((x + b) % 4) + yh)
    pl.semaphore_wait(barrier, 22)

    w_copies = [send(w_h, wy.at[yh], s_w.at[k - 1], r_w.at[k - 1], (tm, 4 * x + (yh + k) % 4))
                for k in range(1, 4)]
    for c in w_copies:
        c.start()
    raw_up = send(raw_h, rleft, s_raw.at[0], r_raw.at[0], (tm, up))
    raw_down = send(raw_h, rright, s_raw.at[1], r_raw.at[1], (tm, down))
    raw_up.start()
    raw_down.start()
    m_copies = [send(mrow, masks.at[g], s_m.at[k - 1], r_m.at[k - 1], (4 * z + (g + k) % 4, depth))
                for k in range(1, 4)]
    for c in m_copies:
        c.start()
    masks[g] = mrow[...]

    loads[0].wait()
    for c in w_copies:
        c.wait()
    parts = [wy[i].astype(F32) for i in range(4)]
    wp[0] = jnp.concatenate([parts[0], parts[1][:, :64]], axis=1).astype(BF)
    wp[1] = jnp.concatenate([parts[1][:, 64:], parts[2][:, :128]], axis=1).astype(BF)
    wp[2] = jnp.concatenate([parts[2][:, 128:], parts[3]], axis=1).astype(BF)
    rows = pl.ds(pl.multiple_of(g * 64, 64), 64)

    def to_all(j, k):
        pair = 3 * x + j
        return send(wp.at[j], wfull.at[z, 0, rows], s_d.at[j, k], r_d.at[g],
                    (4 * z + pair % 4, 4 * ((x + k) % 4) + yh))

    def to_one(j):
        pair = 3 * x + j
        return send(wp.at[j], wfull.at[z, pair // 4, rows], s_e.at[j], r_e.at[pair // 4],
                    (4 * z + pair % 4, 4 * g + yh))

    def keep_query(j):
        return pltpu.make_async_copy(wp.at[j], wfull.at[z, 0, rows], r_d.at[g])

    def keep_other(j):
        pair = 3 * x + j
        return pltpu.make_async_copy(wp.at[j], wfull.at[z, pair // 4, rows], r_e.at[pair // 4])

    def direct(j, act, stay):
        pair = 3 * x + j
        mine = pair % 4 == g

        @pl.when(pair < 4)
        def _():
            for k in range(1, 4):
                act(to_all(j, k))

            @pl.when(mine)
            def _():
                stay(keep_query(j))

            @pl.when(jnp.logical_not(mine))
            def _():
                act(to_all(j, 0))

        @pl.when(pair >= 4)
        def _():
            own = jnp.logical_and(mine, x == g)

            @pl.when(own)
            def _():
                stay(keep_other(j))

            @pl.when(jnp.logical_not(own))
            def _():
                act(to_one(j))

    for j in range(3):
        direct(j, lambda c: c.start(), lambda c: c.start())

    for c in loads[1:]:
        c.wait()
    raw_up.wait()
    raw_down.wait()
    pad[:, 1:9, :] = raw[...].astype(F32)
    pad[:, 0:1, :] = jnp.where(depth == 0, 0.0, rleft[:, 7:8, :].astype(F32))
    pad[:, 9:10, :] = jnp.where(depth == 15, 0.0, rright[:, 0:1, :].astype(F32))
    windows = [pad[:, j:j + 8, :].reshape(128, 128).astype(BF) for j in range(3)]
    squares = jnp.zeros((128, 1), F32)
    for n in range(4):
        cols = slice(512 * n, 512 * n + 512)
        e = stream[:, cols].astype(F32)
        for j in range(3):
            e = e + jnp.dot(windows[j], conv[j, :, cols], preferred_element_type=F32)
        emb[:, cols] = e
        squares = squares + jnp.sum(e * e, axis=-1, keepdims=True)
    inv = lax.rsqrt(squares * (1.0 / 2048) + 1e-05)
    tok[g] = (emb[...] * inv * gain[...]).astype(BF)
    partner = g + 1 - 2 * (g % 2)
    across = (g + 2) % 4
    t_across = send(tok.at[g], tok.at[g], s_t.at[0], r_t.at[0], (4 * z + across, depth))
    t_partner = send(tok.at[g], tok.at[g], s_t.at[1], r_t.at[1], (4 * z + partner, depth))
    t_relay = send(tok.at[across], tok.at[across], s_t.at[2], r_t.at[2], (4 * z + partner, depth))
    t_across.start()
    t_partner.start()

    def half(c, h):
        return wfull.at[c, 0, pl.ds(128 * h, 128)]

    def ring(way, step, h):
        c = (z + 8 - step) % 8 if way == 0 else (z + step) % 8
        i = 2 * step + (h if step < 3 else 0)
        return send(half(c, h), half(c, h), s_z.at[way, i], r_z.at[way, i],
                    (4 * (zr if way == 0 else zl) + g, depth))

    def halves(way, step):
        return (0, 1) if step < 3 else (way,)

    def quarter(c, kinds, at):
        return wfull.at[c, kinds, pl.ds(pl.multiple_of(64 * at, 64), 64)]

    both = pl.ds(1, 2)

    def narrow(way, step):
        c = (z + 8 - step) % 8 if way == 0 else (z + step) % 8
        part = quarter(c, both if step < 3 else pl.ds(1 + way, 1), x)
        return send(part, part, s_b.at[way, step], r_b.at[way, step],
                    (4 * (zr if way == 0 else zl) + g, depth))

    def chunk_of(i):
        return (z + 8 - i) % 8 if i < 4 else (z + i - 3) % 8

    def spread(way, i):
        part = quarter(chunk_of(i), both, x)
        return send(part, part, s_x.at[way, i], r_x.at[way, i], (tm, 4 * (xr if way == 0 else xl) + yh))

    def pass_on(way, i):
        part = quarter(chunk_of(i), pl.ds(1 + way, 1), xl if way == 0 else xr)
        return send(part, part, s_f.at[way, i], r_f.at[way, i], (tm, 4 * (xr if way == 0 else xl) + yh))

    def relay(i):
        for way in (0, 1):
            spread(way, i).wait_recv()
            pass_on(way, i).start()

    def multiply(i):
        c = chunk_of(i)
        cols = pl.ds(pl.multiple_of(c * 256, 256), 256)
        for way in (0, 1):
            pass_on(way, i).wait_recv()

        def one(kind, carry):
            product = jnp.dot(tok[:, :, cols].reshape(512, 256), wfull[c, kind],
                              preferred_element_type=F32)
            acc[kind] = acc[kind] + product if i else product
            return carry

        lax.fori_loop(0, 3, one, 0)

    for kind in (1, 2):
        pltpu.make_async_copy(wp.at[0], quarter(z, kind, x), r_e.at[kind]).wait()
    for way in (0, 1):
        narrow(way, 0).start()
    for way in (0, 1):
        spread(way, 0).start()
    for i in range(4):
        pltpu.make_async_copy(wp.at[0], wfull.at[z, 0, pl.ds(64 * i, 64)], r_d.at[i]).wait()
    for h in (0, 1):
        for way in (0, 1):
            ring(way, 0, h).start()
    for step in range(4):
        for way in (0, 1):
            narrow(way, step).wait_recv()
            if step < 3:
                narrow(way, step + 1).start()
                for to in (0, 1):
                    spread(to, (1 if way == 0 else 4) + step).start()
        if step == 3:
            for to in (0, 1):
                spread(to, 7).start()
        for h in (0, 1):
            for way in (0, 1):
                if h in halves(way, step):
                    ring(way, step, h).wait_recv()
                    if step < 3 and h in halves(way, step + 1):
                        ring(way, step + 1, h).start()
        if step == 0:
            relay(0)
        else:
            relay(step)
            relay(step + 3)
        if step == 1:
            t_across.wait_recv()
            t_relay.start()
        if step == 2:
            t_partner.wait_recv()
            t_relay.wait_recv()
            multiply(0)
            multiply(1)
            multiply(4)
    multiply(2)
    multiply(5)
    relay(7)
    multiply(3)
    multiply(6)
    multiply(7)

    for b in range(4):
        kv[2 + b, :, :256] = acc[1, 128 * b:128 * b + 128].astype(BF)
        kv[2 + b, :, 256:] = acc[2, 128 * b:128 * b + 128].astype(BF)
    kv_ahead = send(kv.at[pl.ds(4, 2)], kv.at[pl.ds(0, 2)], s_kv.at[0], r_kv.at[0], (4 * zr + g, depth))
    kv_back = send(kv.at[pl.ds(2, 2)], kv.at[pl.ds(6, 2)], s_kv.at[1], r_kv.at[1], (4 * zl + g, depth))
    kv_ahead.start()
    kv_back.start()
    for b in range(4):
        q[b] = acc[0, 128 * b:128 * b + 128].astype(BF)
    for c in m_copies:
        c.wait()
    kv_ahead.wait()
    kv_back.wait()

    def attend(b):
        allowed = masks[b][0:1, :] > 0.5
        halves_out = []
        for h in range(2):
            keys = kv[pl.ds(b, 5), :, 128 * h:128 * h + 128].reshape(640, 128)
            values = kv[pl.ds(b, 5), :, 256 + 128 * h:384 + 128 * h].reshape(640, 128)
            query = q[b, :, 128 * h:128 * h + 128]
            scores = lax.dot_general(query, keys, (((1,), (1,)), ((), ())),
                                     preferred_element_type=F32) * (1.0 / math.sqrt(HD))
            scores = jnp.where(allowed, scores, -1e30)
            powers = jnp.exp(scores - jnp.max(scores, axis=-1, keepdims=True))
            weights = (powers / jnp.sum(powers, axis=-1, keepdims=True)).astype(BF)
            halves_out.append(jnp.dot(weights, values, preferred_element_type=F32).astype(BF))
        return halves_out

    def give(k):
        return send(ctx_out.at[k - 1], ctx_in.at[g], s_c.at[k - 1], r_c.at[k - 1],
                    (4 * z + (g + k) % 4, depth))

    for k in (2, 3, 1, 0):
        pieces = attend((g + k) % 4)
        for h in range(2):
            if k:
                ctx_out[k - 1, :, 128 * h:128 * h + 128] = pieces[h]
            else:
                ctx_in[g, :, 128 * h:128 * h + 128] = pieces[h]
        if k:
            give(k).start()

    for j in range(3):
        direct(j, lambda c: c.wait_send(), lambda c: None)
    t_across.wait_send()
    t_partner.wait_send()
    t_relay.wait_send()
    for way in (0, 1):
        for step in range(4):
            for h in halves(way, step):
                ring(way, step, h).wait_send()
            narrow(way, step).wait_send()
        for i in range(8):
            spread(way, i).wait_send()
            pass_on(way, i).wait_send()
    for k in (2, 3, 1):
        give(k).wait()
    for i in range(4):
        out[:, 256 * i:256 * i + 256] = ctx_in[i]


def per_device(raw, stream, conv_w, gain, w_qkv, mask):
    mrow = jnp.broadcast_to(jnp.repeat(mask.reshape(1, 5).astype(F32), 128, axis=1), (8, 640))
    vmem = pltpu.VMEM
    dma = pltpu.SemaphoreType.DMA
    context = pl.pallas_call(
        layer,
        out_shape=jax.ShapeDtypeStruct((128, 1024), BF),
        in_specs=[pl.BlockSpec(memory_space=pl.ANY)] * 5 + [pl.BlockSpec(memory_space=pltpu.VMEM)],
        out_specs=pl.BlockSpec(memory_space=pltpu.VMEM),
        scratch_shapes=[
            vmem((16, 8, 128), BF), vmem((128, 2048), BF), vmem((3, 128, 2048), BF), vmem((1, 2048), F32),
            vmem((16, 16, 128), F32), vmem((16, 8, 128), BF), vmem((16, 8, 128), BF),
            vmem((128, 2048), F32), vmem((4, 128, 2048), BF), vmem((4, 64, 192), BF),
            vmem((3, 64, 256), BF), vmem((8, 3, 256, 256), BF), vmem((3, 512, 256), F32),
            vmem((4, 128, 256), BF), vmem((8, 128, 512), BF), vmem((4, 8, 640), F32),
            vmem((3, 128, 256), BF), vmem((4, 128, 256), BF),
            dma((5,)), dma((3,)), dma((3,)), dma((2,)), dma((2,)), dma((3,)), dma((3,)),
            dma((3, 4)), dma((4,)), dma((3,)), dma((3,)), dma((3,)), dma((3,)),
            dma((2, 7)), dma((2, 7)), dma((2, 4)), dma((2, 4)), dma((2, 8)), dma((2, 8)),
            dma((2, 8)), dma((2, 8)), dma((2,)), dma((2,)), dma((3,)), dma((3,)),
        ],
        compiler_params=pltpu.CompilerParams(
            collective_id=0, has_side_effects=True, vmem_limit_bytes=66_000_000),
    )(raw, stream.reshape(128, 2048), conv_w, gain.reshape(1, 2048), w_qkv, mrow)
    return context.reshape(16, 8, 1024)


def solution(mesh):
    in_specs = (P("tm", "depth", None), P("tm", "depth", None), P(), P(), P("tm", "depth"),
                P("depth", "tm", None))
    return jax.shard_map(per_device, mesh=mesh, in_specs=in_specs,
                         out_specs=P("tm", "depth", None), check_vma=False)
```

```python
import math

import jax
import jax.numpy as jnp
from jax import lax
from jax.experimental import pallas as pl
from jax.experimental.pallas import tpu as pltpu
from jax.sharding import PartitionSpec as P

HEADS = 8
HD = 128
BF = jnp.bfloat16
F32 = jnp.float32


def layer(raw_h, stream_h, conv_h, gain_h, w_h, mask_h, out, raw, stream, conv, gain, pad, rleft, rright,
          emb, tok, wy, wp, wfull, acc, q, kv, masks, ctx_out, ctx_in, s_in, s_w, r_w, s_raw, r_raw,
          s_m, r_m, s_d, r_d, s_e, r_e, s_t, r_t, s_z, r_z, s_b, r_b, s_x, r_x, s_f, r_f, s_kv, r_kv,
          s_c, r_c):
    tm, depth = lax.axis_index("tm"), lax.axis_index("depth")
    z, g = tm // 4, tm % 4
    x, yh = depth // 4, depth % 4
    up, down = (depth + 1) % 16, (depth + 15) % 16
    zr, zl = (z + 1) % 8, (z + 7) % 8
    xr, xl = (x + 1) % 4, (x + 3) % 4

    loads = [pltpu.make_async_copy(a, b, s_in.at[i]) for i, (a, b) in enumerate(
        ((w_h, wy.at[yh]), (raw_h, raw), (conv_h, conv), (stream_h, stream), (gain_h, gain),
         (mask_h, masks.at[g])))]
    for c in loads:
        c.start()

    def send(src, dst, s, r, to):
        return pltpu.make_async_remote_copy(
            src_ref=src, dst_ref=dst, send_sem=s, recv_sem=r, device_id=to,
            device_id_type=pl.DeviceIdType.MESH)

    barrier = pltpu.get_barrier_semaphore()

    def greet(a, b):
        pl.semaphore_signal(barrier, inc=1, device_id=(a, b), device_id_type=pl.DeviceIdType.MESH)

    for k in range(1, 4):
        greet(tm, 4 * x + (yh + k) % 4)
    greet(tm, up)
    greet(tm, down)
    greet(4 * zr + g, depth)
    greet(4 * zl + g, depth)
    for a in range(4):
        for b in range(4):
            if a or b:
                greet(4 * z + (g + a) % 4, 4 * ((x + b) % 4) + yh)
    pl.semaphore_wait(barrier, 22)

    w_copies = [send(w_h, wy.at[yh], s_w.at[k - 1], r_w.at[k - 1], (tm, 4 * x + (yh + k) % 4))
                for k in range(1, 4)]
    for c in w_copies:
        c.start()
    raw_up = send(raw_h, rleft, s_raw.at[0], r_raw.at[0], (tm, up))
    raw_down = send(raw_h, rright, s_raw.at[1], r_raw.at[1], (tm, down))
    raw_up.start()
    raw_down.start()
    m_copies = [send(mask_h, masks.at[g], s_m.at[k - 1], r_m.at[k - 1], (4 * z + (g + k) % 4, depth))
                for k in range(1, 4)]
    for c in m_copies:
        c.start()

    loads[0].wait()
    for c in w_copies:
        c.wait()
    parts = [wy[i].astype(F32) for i in range(4)]
    wp[0] = jnp.concatenate([parts[0], parts[1][:, :64]], axis=1).astype(BF)
    wp[1] = jnp.concatenate([parts[1][:, 64:], parts[2][:, :128]], axis=1).astype(BF)
    wp[2] = jnp.concatenate([parts[2][:, 128:], parts[3]], axis=1).astype(BF)
    rows = pl.ds(pl.multiple_of(g * 64, 64), 64)

    def to_all(j, k):
        pair = 3 * x + j
        return send(wp.at[j], wfull.at[z, 0, rows], s_d.at[j, k], r_d.at[g],
                    (4 * z + pair % 4, 4 * ((x + k) % 4) + yh))

    def to_one(j):
        pair = 3 * x + j
        return send(wp.at[j], wfull.at[z, pair // 4, rows], s_e.at[j], r_e.at[pair // 4],
                    (4 * z + pair % 4, 4 * g + yh))

    def keep_query(j):
        return pltpu.make_async_copy(wp.at[j], wfull.at[z, 0, rows], r_d.at[g])

    def keep_other(j):
        pair = 3 * x + j
        return pltpu.make_async_copy(wp.at[j], wfull.at[z, pair // 4, rows], r_e.at[pair // 4])

    def direct(j, act, stay):
        pair = 3 * x + j
        mine = pair % 4 == g

        @pl.when(pair < 4)
        def _():
            for k in range(1, 4):
                act(to_all(j, k))

            @pl.when(mine)
            def _():
                stay(keep_query(j))

            @pl.when(jnp.logical_not(mine))
            def _():
                act(to_all(j, 0))

        @pl.when(pair >= 4)
        def _():
            own = jnp.logical_and(mine, x == g)

            @pl.when(own)
            def _():
                stay(keep_other(j))

            @pl.when(jnp.logical_not(own))
            def _():
                act(to_one(j))

    for j in range(3):
        direct(j, lambda c: c.start(), lambda c: c.start())

    for c in loads[1:]:
        c.wait()
    raw_up.wait()
    raw_down.wait()
    pad[:, 1:9, :] = raw[...].astype(F32)
    pad[:, 0:1, :] = jnp.where(depth == 0, 0.0, rleft[:, 7:8, :].astype(F32))
    pad[:, 9:10, :] = jnp.where(depth == 15, 0.0, rright[:, 0:1, :].astype(F32))
    windows = [pad[:, j:j + 8, :].reshape(128, 128).astype(BF) for j in range(3)]
    squares = jnp.zeros((128, 1), F32)
    for n in range(4):
        cols = slice(512 * n, 512 * n + 512)
        e = stream[:, cols].astype(F32)
        for j in range(3):
            e = e + jnp.dot(windows[j], conv[j, :, cols], preferred_element_type=F32)
        emb[:, cols] = e
        squares = squares + jnp.sum(e * e, axis=-1, keepdims=True)
    inv = lax.rsqrt(squares * (1.0 / 2048) + 1e-05)
    tok[g] = (emb[...] * inv * gain[...]).astype(BF)
    partner = g + 1 - 2 * (g % 2)
    across = (g + 2) % 4
    t_across = send(tok.at[g], tok.at[g], s_t.at[0], r_t.at[0], (4 * z + across, depth))
    t_partner = send(tok.at[g], tok.at[g], s_t.at[1], r_t.at[1], (4 * z + partner, depth))
    t_relay = send(tok.at[across], tok.at[across], s_t.at[2], r_t.at[2], (4 * z + partner, depth))
    t_across.start()
    t_partner.start()

    def half(c, h):
        return wfull.at[c, 0, pl.ds(128 * h, 128)]

    def ring(way, step, h):
        c = (z + 8 - step) % 8 if way == 0 else (z + step) % 8
        i = 2 * step + (h if step < 3 else 0)
        return send(half(c, h), half(c, h), s_z.at[way, i], r_z.at[way, i],
                    (4 * (zr if way == 0 else zl) + g, depth))

    def halves(way, step):
        return (0, 1) if step < 3 else (way,)

    def quarter(c, kinds, at):
        return wfull.at[c, kinds, pl.ds(pl.multiple_of(64 * at, 64), 64)]

    both = pl.ds(1, 2)

    def narrow(way, step):
        c = (z + 8 - step) % 8 if way == 0 else (z + step) % 8
        part = quarter(c, both if step < 3 else pl.ds(1 + way, 1), x)
        return send(part, part, s_b.at[way, step], r_b.at[way, step],
                    (4 * (zr if way == 0 else zl) + g, depth))

    def chunk_of(i):
        return (z + 8 - i) % 8 if i < 4 else (z + i - 3) % 8

    def spread(way, i):
        part = quarter(chunk_of(i), both, x)
        return send(part, part, s_x.at[way, i], r_x.at[way, i], (tm, 4 * (xr if way == 0 else xl) + yh))

    def pass_on(way, i):
        part = quarter(chunk_of(i), pl.ds(1 + way, 1), xl if way == 0 else xr)
        return send(part, part, s_f.at[way, i], r_f.at[way, i], (tm, 4 * (xr if way == 0 else xl) + yh))

    def relay(i):
        for way in (0, 1):
            spread(way, i).wait_recv()
            pass_on(way, i).start()

    def multiply(i):
        c = chunk_of(i)
        cols = pl.ds(pl.multiple_of(c * 256, 256), 256)
        for way in (0, 1):
            pass_on(way, i).wait_recv()

        def one(kind, carry):
            product = jnp.dot(tok[:, :, cols].reshape(512, 256), wfull[c, kind],
                              preferred_element_type=F32)
            acc[kind] = acc[kind] + product if i else product
            return carry

        lax.fori_loop(0, 3, one, 0)

    for kind in (1, 2):
        pltpu.make_async_copy(wp.at[0], quarter(z, kind, x), r_e.at[kind]).wait()
    for way in (0, 1):
        narrow(way, 0).start()
    for way in (0, 1):
        spread(way, 0).start()
    for i in range(4):
        pltpu.make_async_copy(wp.at[0], wfull.at[z, 0, pl.ds(64 * i, 64)], r_d.at[i]).wait()
    for h in (0, 1):
        for way in (0, 1):
            ring(way, 0, h).start()
    for step in range(4):
        for way in (0, 1):
            narrow(way, step).wait_recv()
            if step < 3:
                narrow(way, step + 1).start()
                for to in (0, 1):
                    spread(to, (1 if way == 0 else 4) + step).start()
        if step == 3:
            for to in (0, 1):
                spread(to, 7).start()
        for h in (0, 1):
            for way in (0, 1):
                if h in halves(way, step):
                    ring(way, step, h).wait_recv()
                    if step < 3 and h in halves(way, step + 1):
                        ring(way, step + 1, h).start()
        if step == 0:
            relay(0)
        else:
            relay(step)
            relay(step + 3)
        if step == 2:
            t_across.wait_recv()
            t_relay.start()
            t_partner.wait_recv()
    t_relay.wait_recv()
    for i in (0, 1, 4, 2, 5, 3, 6):
        multiply(i)
        if i == 1:
            relay(7)
    multiply(7)

    for b in range(4):
        kv[2 + b, :, :256] = acc[1, 128 * b:128 * b + 128].astype(BF)
        kv[2 + b, :, 256:] = acc[2, 128 * b:128 * b + 128].astype(BF)
    kv_ahead = send(kv.at[pl.ds(4, 2)], kv.at[pl.ds(0, 2)], s_kv.at[0], r_kv.at[0], (4 * zr + g, depth))
    kv_back = send(kv.at[pl.ds(2, 2)], kv.at[pl.ds(6, 2)], s_kv.at[1], r_kv.at[1], (4 * zl + g, depth))
    kv_ahead.start()
    kv_back.start()
    for b in range(4):
        q[b] = acc[0, 128 * b:128 * b + 128].astype(BF)
    for c in m_copies:
        c.wait()
    kv_ahead.wait()
    kv_back.wait()

    def attend(b):
        row = masks[b]
        allowed = jnp.concatenate([jnp.broadcast_to(row[:, e:e + 1], (1, 128)) for e in range(5)], axis=1) > 0
        halves_out = []
        for h in range(2):
            keys = kv[pl.ds(b, 5), :, 128 * h:128 * h + 128].reshape(640, 128)
            values = kv[pl.ds(b, 5), :, 256 + 128 * h:384 + 128 * h].reshape(640, 128)
            query = q[b, :, 128 * h:128 * h + 128]
            scores = lax.dot_general(query, keys, (((1,), (1,)), ((), ())),
                                     preferred_element_type=F32) * (1.0 / math.sqrt(HD))
            scores = jnp.where(allowed, scores, -1e30)
            powers = jnp.exp(scores - jnp.max(scores, axis=-1, keepdims=True))
            weights = (powers / jnp.sum(powers, axis=-1, keepdims=True)).astype(BF)
            halves_out.append(jnp.dot(weights, values, preferred_element_type=F32).astype(BF))
        return halves_out

    def give(k):
        return send(ctx_out.at[k - 1], ctx_in.at[g], s_c.at[k - 1], r_c.at[k - 1],
                    (4 * z + (g + k) % 4, depth))

    for k in (2, 3, 1, 0):
        pieces = attend((g + k) % 4)
        for h in range(2):
            if k:
                ctx_out[k - 1, :, 128 * h:128 * h + 128] = pieces[h]
            else:
                ctx_in[g, :, 128 * h:128 * h + 128] = pieces[h]
        if k:
            give(k).start()

    for j in range(3):
        direct(j, lambda c: c.wait_send(), lambda c: None)
    t_across.wait_send()
    t_partner.wait_send()
    t_relay.wait_send()
    for way in (0, 1):
        for step in range(4):
            for h in halves(way, step):
                ring(way, step, h).wait_send()
            narrow(way, step).wait_send()
        for i in range(8):
            spread(way, i).wait_send()
            pass_on(way, i).wait_send()
    for k in (2, 3, 1):
        give(k).wait()
    for i in range(4):
        out[:, 256 * i:256 * i + 256] = ctx_in[i]


def per_device(raw, stream, conv_w, gain, w_qkv, mask):
    vmem = pltpu.VMEM
    dma = pltpu.SemaphoreType.DMA
    context = pl.pallas_call(
        layer,
        out_shape=jax.ShapeDtypeStruct((128, 1024), BF),
        in_specs=[pl.BlockSpec(memory_space=pltpu.HBM)] * 6,
        out_specs=pl.BlockSpec(memory_space=pltpu.VMEM),
        scratch_shapes=[
            vmem((16, 8, 128), BF), vmem((128, 2048), BF), vmem((3, 128, 2048), BF), vmem((1, 2048), F32),
            vmem((16, 16, 128), F32), vmem((16, 8, 128), BF), vmem((16, 8, 128), BF),
            vmem((128, 2048), F32), vmem((4, 128, 2048), BF), vmem((4, 64, 192), BF),
            vmem((3, 64, 256), BF), vmem((8, 3, 256, 256), BF), vmem((3, 512, 256), F32),
            vmem((4, 128, 256), BF), vmem((8, 128, 512), BF), vmem((4, 1, 5), jnp.int32),
            vmem((3, 128, 256), BF), vmem((4, 128, 256), BF),
            dma((6,)), dma((3,)), dma((3,)), dma((2,)), dma((2,)), dma((3,)), dma((3,)),
            dma((3, 4)), dma((4,)), dma((3,)), dma((3,)), dma((3,)), dma((3,)),
            dma((2, 7)), dma((2, 7)), dma((2, 4)), dma((2, 4)), dma((2, 8)), dma((2, 8)),
            dma((2, 8)), dma((2, 8)), dma((2,)), dma((2,)), dma((3,)), dma((3,)),
        ],
        compiler_params=pltpu.CompilerParams(
            collective_id=0, has_side_effects=True, vmem_limit_bytes=48 * 1024 * 1024),
    )(*[pltpu.with_memory_space_constraint(a, pltpu.HBM) for a in (
        raw, stream.reshape(128, 2048), conv_w, gain.reshape(1, 2048), w_qkv, mask.reshape(1, 5))])
    return context.reshape(16, 8, 1024)


def solution(mesh):
    in_specs = (P("tm", "depth", None), P("tm", "depth", None), P(), P(), P("tm", "depth"),
                P("depth", "tm", None))
    return jax.shard_map(per_device, mesh=mesh, in_specs=in_specs,
                         out_specs=P("tm", "depth", None), check_vma=False)
```

```python
import math

import jax
import jax.numpy as jnp
from jax import lax
from jax.experimental import pallas as pl
from jax.experimental.pallas import tpu as pltpu
from jax.sharding import PartitionSpec as P

HEADS = 8
HD = 128
BF = jnp.bfloat16
F32 = jnp.float32


def layer(raw_h, stream_h, conv_h, gain_h, w_h, mask_h, out, raw, stream, conv, gain, pad, rleft, rright,
          emb, tok, wy, wp, wfull, acc, q, kv, masks, ctx_out, ctx_in, s_in, s_w, r_w, s_raw, r_raw,
          s_m, r_m, s_d, r_d, s_e, r_e, s_t, r_t, s_z, r_z, s_b, r_b, s_x, r_x, s_f, r_f, s_kv, r_kv,
          s_c, r_c):
    tm, depth = lax.axis_index("tm"), lax.axis_index("depth")
    z, g = tm // 4, tm % 4
    x, yh = depth // 4, depth % 4
    up, down = (depth + 1) % 16, (depth + 15) % 16
    zr, zl = (z + 1) % 8, (z + 7) % 8
    xr, xl = (x + 1) % 4, (x + 3) % 4

    loads = [pltpu.make_async_copy(a, b, s_in.at[i]) for i, (a, b) in enumerate(
        ((w_h, wy.at[yh]), (raw_h, raw), (conv_h, conv), (stream_h, stream), (gain_h, gain),
         (mask_h, masks.at[g])))]
    for c in loads:
        c.start()

    def send(src, dst, s, r, to):
        return pltpu.make_async_remote_copy(
            src_ref=src, dst_ref=dst, send_sem=s, recv_sem=r, device_id=to,
            device_id_type=pl.DeviceIdType.MESH)

    barrier = pltpu.get_barrier_semaphore()

    def greet(a, b):
        pl.semaphore_signal(barrier, inc=1, device_id=(a, b), device_id_type=pl.DeviceIdType.MESH)

    for k in range(1, 4):
        greet(tm, 4 * x + (yh + k) % 4)
    greet(tm, up)
    greet(tm, down)
    greet(4 * zr + g, depth)
    greet(4 * zl + g, depth)
    for a in range(4):
        for b in range(4):
            if a or b:
                greet(4 * z + (g + a) % 4, 4 * ((x + b) % 4) + yh)
    pl.semaphore_wait(barrier, 22)

    w_copies = [send(w_h, wy.at[yh], s_w.at[k - 1], r_w.at[k - 1], (tm, 4 * x + (yh + k) % 4))
                for k in range(1, 4)]
    for c in w_copies:
        c.start()
    raw_up = send(raw_h, rleft, s_raw.at[0], r_raw.at[0], (tm, up))
    raw_down = send(raw_h, rright, s_raw.at[1], r_raw.at[1], (tm, down))
    raw_up.start()
    raw_down.start()
    m_copies = [send(mask_h, masks.at[g], s_m.at[k - 1], r_m.at[k - 1], (4 * z + (g + k) % 4, depth))
                for k in range(1, 4)]
    for c in m_copies:
        c.start()

    loads[0].wait()
    for c in w_copies:
        c.wait()
    parts = [wy[i].astype(F32) for i in range(4)]
    wp[0] = jnp.concatenate([parts[0], parts[1][:, :64]], axis=1).astype(BF)
    wp[1] = jnp.concatenate([parts[1][:, 64:], parts[2][:, :128]], axis=1).astype(BF)
    wp[2] = jnp.concatenate([parts[2][:, 128:], parts[3]], axis=1).astype(BF)
    rows = pl.ds(pl.multiple_of(g * 64, 64), 64)

    def to_all(j, k):
        pair = 3 * x + j
        return send(wp.at[j], wfull.at[z, 0, rows], s_d.at[j, k], r_d.at[g],
                    (4 * z + pair % 4, 4 * ((x + k) % 4) + yh))

    def to_one(j):
        pair = 3 * x + j
        return send(wp.at[j], wfull.at[z, pair // 4, rows], s_e.at[j], r_e.at[pair // 4],
                    (4 * z + pair % 4, 4 * g + yh))

    def keep_query(j):
        return pltpu.make_async_copy(wp.at[j], wfull.at[z, 0, rows], r_d.at[g])

    def keep_other(j):
        pair = 3 * x + j
        return pltpu.make_async_copy(wp.at[j], wfull.at[z, pair // 4, rows], r_e.at[pair // 4])

    def direct(j, act, stay):
        pair = 3 * x + j
        mine = pair % 4 == g

        @pl.when(pair < 4)
        def _():
            for k in range(1, 4):
                act(to_all(j, k))

            @pl.when(mine)
            def _():
                stay(keep_query(j))

            @pl.when(jnp.logical_not(mine))
            def _():
                act(to_all(j, 0))

        @pl.when(pair >= 4)
        def _():
            own = jnp.logical_and(mine, x == g)

            @pl.when(own)
            def _():
                stay(keep_other(j))

            @pl.when(jnp.logical_not(own))
            def _():
                act(to_one(j))

    for j in range(3):
        direct(j, lambda c: c.start(), lambda c: c.start())

    for c in loads[1:]:
        c.wait()
    raw_up.wait()
    raw_down.wait()
    pad[:, 1:9, :] = raw[...].astype(F32)
    pad[:, 0:1, :] = jnp.where(depth == 0, 0.0, rleft[:, 7:8, :].astype(F32))
    pad[:, 9:10, :] = jnp.where(depth == 15, 0.0, rright[:, 0:1, :].astype(F32))
    windows = [pad[:, j:j + 8, :].reshape(128, 128).astype(BF) for j in range(3)]
    squares = jnp.zeros((128, 1), F32)
    for n in range(4):
        cols = slice(512 * n, 512 * n + 512)
        e = stream[:, cols].astype(F32)
        for j in range(3):
            e = e + jnp.dot(windows[j], conv[j, :, cols], preferred_element_type=F32)
        emb[:, cols] = e
        squares = squares + jnp.sum(e * e, axis=-1, keepdims=True)
    inv = lax.rsqrt(squares * (1.0 / 2048) + 1e-05)
    tok[g] = (emb[...] * inv * gain[...]).astype(BF)
    partner = g + 1 - 2 * (g % 2)
    across = (g + 2) % 4
    t_across = send(tok.at[g], tok.at[g], s_t.at[0], r_t.at[0], (4 * z + across, depth))
    t_partner = send(tok.at[g], tok.at[g], s_t.at[1], r_t.at[1], (4 * z + partner, depth))
    t_relay = send(tok.at[across], tok.at[across], s_t.at[2], r_t.at[2], (4 * z + partner, depth))
    t_across.start()
    t_partner.start()

    def half(c, h):
        return wfull.at[c, 0, pl.ds(128 * h, 128)]

    def ring(way, step, h):
        c = (z + 8 - step) % 8 if way == 0 else (z + step) % 8
        i = 2 * step + (h if step < 3 else 0)
        return send(half(c, h), half(c, h), s_z.at[way, i], r_z.at[way, i],
                    (4 * (zr if way == 0 else zl) + g, depth))

    def halves(way, step):
        return (0, 1) if step < 3 else (way,)

    def quarter(c, kinds, at):
        return wfull.at[c, kinds, pl.ds(pl.multiple_of(64 * at, 64), 64)]

    both = pl.ds(1, 2)

    def narrow(way, step):
        c = (z + 8 - step) % 8 if way == 0 else (z + step) % 8
        part = quarter(c, both if step < 3 else pl.ds(1 + way, 1), x)
        return send(part, part, s_b.at[way, step], r_b.at[way, step],
                    (4 * (zr if way == 0 else zl) + g, depth))

    def chunk_of(i):
        return (z + 8 - i) % 8 if i < 4 else (z + i - 3) % 8

    def spread(way, i):
        part = quarter(chunk_of(i), both, x)
        return send(part, part, s_x.at[way, i], r_x.at[way, i], (tm, 4 * (xr if way == 0 else xl) + yh))

    def pass_on(way, i):
        part = quarter(chunk_of(i), pl.ds(1 + way, 1), xl if way == 0 else xr)
        return send(part, part, s_f.at[way, i], r_f.at[way, i], (tm, 4 * (xr if way == 0 else xl) + yh))

    def relay(i):
        for way in (0, 1):
            spread(way, i).wait_recv()
            pass_on(way, i).start()

    near, far = 2 * (g // 2), 2 - 2 * (g // 2)

    def multiply(i, first, kind, base, count):
        c = chunk_of(i)
        cols = pl.ds(pl.multiple_of(c * 256, 256), 256)
        who = pl.ds(base, count)
        product = jnp.dot(tok[who, :, cols].reshape(128 * count, 256), wfull[c, kind],
                          preferred_element_type=F32).reshape(count, 128, 256)
        acc[kind, who] = product if first else acc[kind, who] + product

    def others(i, base, count):
        lax.fori_loop(1, 3, lambda kind, t: multiply(i, i == 0, kind, base, count), None)

    def landed(i):
        for way in (0, 1):
            pass_on(way, i).wait_recv()

    for kind in (1, 2):
        pltpu.make_async_copy(wp.at[0], quarter(z, kind, x), r_e.at[kind]).wait()
    for way in (0, 1):
        narrow(way, 0).start()
    for way in (0, 1):
        spread(way, 0).start()
    for i in range(4):
        pltpu.make_async_copy(wp.at[0], wfull.at[z, 0, pl.ds(64 * i, 64)], r_d.at[i]).wait()
    for h in (0, 1):
        for way in (0, 1):
            ring(way, 0, h).start()
    for step in range(4):
        for way in (0, 1):
            narrow(way, step).wait_recv()
            if step < 3:
                narrow(way, step + 1).start()
                for to in (0, 1):
                    spread(to, (1 if way == 0 else 4) + step).start()
        if step == 3:
            for to in (0, 1):
                spread(to, 7).start()
        for h in (0, 1):
            for way in (0, 1):
                if h in halves(way, step):
                    ring(way, step, h).wait_recv()
                    if step < 3 and h in halves(way, step + 1):
                        ring(way, step + 1, h).start()
        if step == 0:
            relay(0)
        else:
            relay(step)
            relay(step + 3)
        if step == 1:
            t_partner.wait_recv()
            landed(0)
            others(0, near, 2)
        if step == 2:
            t_across.wait_recv()
            t_relay.start()
            landed(1)
            others(1, near, 2)
            landed(4)
            others(4, near, 2)
    for i in (2, 5):
        landed(i)
        others(i, near, 2)
    relay(7)
    t_relay.wait_recv()
    for i in (0, 1, 4, 2, 5):
        others(i, far, 2)
    for i in (3, 6, 7):
        landed(i)
        others(i, 0, 4)

    for b in range(4):
        kv[2 + b, :, :256] = acc[1, b].astype(BF)
        kv[2 + b, :, 256:] = acc[2, b].astype(BF)
    kv_ahead = send(kv.at[pl.ds(4, 2)], kv.at[pl.ds(0, 2)], s_kv.at[0], r_kv.at[0], (4 * zr + g, depth))
    kv_back = send(kv.at[pl.ds(2, 2)], kv.at[pl.ds(6, 2)], s_kv.at[1], r_kv.at[1], (4 * zl + g, depth))
    kv_ahead.start()
    kv_back.start()
    for i in range(8):
        multiply(i, i == 0, 0, 0, 4)
    q[...] = acc[0].astype(BF)
    for c in m_copies:
        c.wait()
    kv_ahead.wait()
    kv_back.wait()

    def attend(b):
        row = masks[b]
        allowed = jnp.concatenate([jnp.broadcast_to(row[:, e:e + 1], (1, 128)) for e in range(5)], axis=1) > 0
        halves_out = []
        for h in range(2):
            keys = kv[pl.ds(b, 5), :, 128 * h:128 * h + 128].reshape(640, 128)
            values = kv[pl.ds(b, 5), :, 256 + 128 * h:384 + 128 * h].reshape(640, 128)
            query = q[b, :, 128 * h:128 * h + 128]
            scores = lax.dot_general(query, keys, (((1,), (1,)), ((), ())),
                                     preferred_element_type=F32) * (1.0 / math.sqrt(HD))
            scores = jnp.where(allowed, scores, -1e30)
            powers = jnp.exp(scores - jnp.max(scores, axis=-1, keepdims=True))
            weights = (powers / jnp.sum(powers, axis=-1, keepdims=True)).astype(BF)
            halves_out.append(jnp.dot(weights, values, preferred_element_type=F32).astype(BF))
        return halves_out

    def give(k):
        return send(ctx_out.at[k - 1], ctx_in.at[g], s_c.at[k - 1], r_c.at[k - 1],
                    (4 * z + (g + k) % 4, depth))

    for k in (2, 3, 1, 0):
        pieces = attend((g + k) % 4)
        for h in range(2):
            if k:
                ctx_out[k - 1, :, 128 * h:128 * h + 128] = pieces[h]
            else:
                ctx_in[g, :, 128 * h:128 * h + 128] = pieces[h]
        if k:
            give(k).start()

    for j in range(3):
        direct(j, lambda c: c.wait_send(), lambda c: None)
    t_across.wait_send()
    t_partner.wait_send()
    t_relay.wait_send()
    for way in (0, 1):
        for step in range(4):
            for h in halves(way, step):
                ring(way, step, h).wait_send()
            narrow(way, step).wait_send()
        for i in range(8):
            spread(way, i).wait_send()
            pass_on(way, i).wait_send()
    for k in (2, 3, 1):
        give(k).wait()
    for i in range(4):
        out[:, 256 * i:256 * i + 256] = ctx_in[i]


def per_device(raw, stream, conv_w, gain, w_qkv, mask):
    vmem = pltpu.VMEM
    dma = pltpu.SemaphoreType.DMA
    context = pl.pallas_call(
        layer,
        out_shape=jax.ShapeDtypeStruct((128, 1024), BF),
        in_specs=[pl.BlockSpec(memory_space=pltpu.HBM)] * 6,
        out_specs=pl.BlockSpec(memory_space=pltpu.VMEM),
        scratch_shapes=[
            vmem((16, 8, 128), BF), vmem((128, 2048), BF), vmem((3, 128, 2048), BF), vmem((1, 2048), F32),
            vmem((16, 16, 128), F32), vmem((16, 8, 128), BF), vmem((16, 8, 128), BF),
            vmem((128, 2048), F32), vmem((4, 128, 2048), BF), vmem((4, 64, 192), BF),
            vmem((3, 64, 256), BF), vmem((8, 3, 256, 256), BF), vmem((3, 4, 128, 256), F32),
            vmem((4, 128, 256), BF), vmem((8, 128, 512), BF), vmem((4, 1, 5), jnp.int32),
            vmem((3, 128, 256), BF), vmem((4, 128, 256), BF),
            dma((6,)), dma((3,)), dma((3,)), dma((2,)), dma((2,)), dma((3,)), dma((3,)),
            dma((3, 4)), dma((4,)), dma((3,)), dma((3,)), dma((3,)), dma((3,)),
            dma((2, 7)), dma((2, 7)), dma((2, 4)), dma((2, 4)), dma((2, 8)), dma((2, 8)),
            dma((2, 8)), dma((2, 8)), dma((2,)), dma((2,)), dma((3,)), dma((3,)),
        ],
        compiler_params=pltpu.CompilerParams(
            collective_id=0, has_side_effects=True, vmem_limit_bytes=48 * 1024 * 1024),
    )(*[pltpu.with_memory_space_constraint(a, pltpu.HBM) for a in (
        raw, stream.reshape(128, 2048), conv_w, gain.reshape(1, 2048), w_qkv, mask.reshape(1, 5))])
    return context.reshape(16, 8, 1024)


def solution(mesh):
    in_specs = (P("tm", "depth", None), P("tm", "depth", None), P(), P(), P("tm", "depth"),
                P("depth", "tm", None))
    return jax.shard_map(per_device, mesh=mesh, in_specs=in_specs,
                         out_specs=P("tm", "depth", None), check_vma=False)
```

```python
import math

import jax
import jax.numpy as jnp
from jax import lax
from jax.experimental import pallas as pl
from jax.experimental.pallas import tpu as pltpu
from jax.sharding import PartitionSpec as P

HEADS = 8
HD = 128
BF = jnp.bfloat16
F32 = jnp.float32


def layer(raw_h, stream_h, conv_h, gain_h, w_h, mask_h, out, raw, stream, conv, gain, pad, rleft, rright,
          emb, tok, wy, wp, wfull, acc, q, kv, masks, ctx_out, ctx_in, s_in, s_w, r_w, s_raw, r_raw,
          s_m, r_m, s_d, r_d, s_e, r_e, s_t, r_t, s_z, r_z, s_b, r_b, s_x, r_x, s_f, r_f, s_kv, r_kv,
          s_c, r_c):
    tm, depth = lax.axis_index("tm"), lax.axis_index("depth")
    z, g = tm // 4, tm % 4
    x, yh = depth // 4, depth % 4
    up, down = (depth + 1) % 16, (depth + 15) % 16
    zr, zl = (z + 1) % 8, (z + 7) % 8
    xr, xl = (x + 1) % 4, (x + 3) % 4

    loads = [pltpu.make_async_copy(a, b, s_in.at[i]) for i, (a, b) in enumerate(
        ((w_h, wy.at[yh]), (raw_h, raw), (conv_h, conv), (stream_h, stream), (gain_h, gain),
         (mask_h, masks.at[g])))]
    for c in loads:
        c.start()

    def send(src, dst, s, r, to):
        return pltpu.make_async_remote_copy(
            src_ref=src, dst_ref=dst, send_sem=s, recv_sem=r, device_id=to,
            device_id_type=pl.DeviceIdType.MESH)

    barrier = pltpu.get_barrier_semaphore()

    def greet(a, b):
        pl.semaphore_signal(barrier, inc=1, device_id=(a, b), device_id_type=pl.DeviceIdType.MESH)

    for k in range(1, 4):
        greet(tm, 4 * x + (yh + k) % 4)
    greet(tm, up)
    greet(tm, down)
    greet(4 * zr + g, depth)
    greet(4 * zl + g, depth)
    for a in range(4):
        for b in range(4):
            if a or b:
                greet(4 * z + (g + a) % 4, 4 * ((x + b) % 4) + yh)
    pl.semaphore_wait(barrier, 22)

    w_copies = [send(w_h, wy.at[yh], s_w.at[k - 1], r_w.at[k - 1], (tm, 4 * x + (yh + k) % 4))
                for k in range(1, 4)]
    for c in w_copies:
        c.start()
    raw_up = send(raw_h, rleft, s_raw.at[0], r_raw.at[0], (tm, up))
    raw_down = send(raw_h, rright, s_raw.at[1], r_raw.at[1], (tm, down))
    raw_up.start()
    raw_down.start()
    m_copies = [send(mask_h, masks.at[g], s_m.at[k - 1], r_m.at[k - 1], (4 * z + (g + k) % 4, depth))
                for k in range(1, 4)]
    for c in m_copies:
        c.start()

    loads[0].wait()
    for c in w_copies:
        c.wait()
    parts = [wy[i].astype(F32) for i in range(4)]
    wp[0] = jnp.concatenate([parts[0], parts[1][:, :64]], axis=1).astype(BF)
    wp[1] = jnp.concatenate([parts[1][:, 64:], parts[2][:, :128]], axis=1).astype(BF)
    wp[2] = jnp.concatenate([parts[2][:, 128:], parts[3]], axis=1).astype(BF)
    rows = pl.ds(pl.multiple_of(g * 64, 64), 64)

    def to_all(j, k):
        pair = 3 * x + j
        return send(wp.at[j], wfull.at[z, 1, rows], s_d.at[j, k], r_d.at[g],
                    (4 * z + pair % 4, 4 * ((x + k) % 4) + yh))

    def to_one(j):
        pair = 3 * x + j
        return send(wp.at[j], wfull.at[z, pair // 4, rows], s_e.at[j], r_e.at[pair // 4],
                    (4 * z + pair % 4, 4 * g + yh))

    def keep_key(j):
        return pltpu.make_async_copy(wp.at[j], wfull.at[z, 1, rows], r_d.at[g])

    def keep_other(j):
        pair = 3 * x + j
        return pltpu.make_async_copy(wp.at[j], wfull.at[z, pair // 4, rows], r_e.at[pair // 4])

    def direct(j, act, stay):
        pair = 3 * x + j
        mine = pair % 4 == g

        @pl.when(pair // 4 == 1)
        def _():
            for k in range(1, 4):
                act(to_all(j, k))

            @pl.when(mine)
            def _():
                stay(keep_key(j))

            @pl.when(jnp.logical_not(mine))
            def _():
                act(to_all(j, 0))

        @pl.when(pair // 4 != 1)
        def _():
            own = jnp.logical_and(mine, x == g)

            @pl.when(own)
            def _():
                stay(keep_other(j))

            @pl.when(jnp.logical_not(own))
            def _():
                act(to_one(j))

    for j in range(3):
        direct(j, lambda c: c.start(), lambda c: c.start())

    for c in loads[1:]:
        c.wait()
    raw_up.wait()
    raw_down.wait()
    pad[:, 1:9, :] = raw[...].astype(F32)
    pad[:, 0:1, :] = jnp.where(depth == 0, 0.0, rleft[:, 7:8, :].astype(F32))
    pad[:, 9:10, :] = jnp.where(depth == 15, 0.0, rright[:, 0:1, :].astype(F32))
    windows = [pad[:, j:j + 8, :].reshape(128, 128).astype(BF) for j in range(3)]
    squares = jnp.zeros((128, 1), F32)
    for n in range(4):
        cols = slice(512 * n, 512 * n + 512)
        e = stream[:, cols].astype(F32)
        for j in range(3):
            e = e + jnp.dot(windows[j], conv[j, :, cols], preferred_element_type=F32)
        emb[:, cols] = e
        squares = squares + jnp.sum(e * e, axis=-1, keepdims=True)
    inv = lax.rsqrt(squares * (1.0 / 2048) + 1e-05)
    tok[g] = (emb[...] * inv * gain[...]).astype(BF)
    partner = g + 1 - 2 * (g % 2)
    across = (g + 2) % 4
    t_across = send(tok.at[g], tok.at[g], s_t.at[0], r_t.at[0], (4 * z + across, depth))
    t_partner = send(tok.at[g], tok.at[g], s_t.at[1], r_t.at[1], (4 * z + partner, depth))
    t_relay = send(tok.at[across], tok.at[across], s_t.at[2], r_t.at[2], (4 * z + partner, depth))
    t_across.start()
    t_partner.start()

    def half(c, h):
        return wfull.at[c, 1, pl.ds(128 * h, 128)]

    def ring(way, step, h):
        c = (z + 8 - step) % 8 if way == 0 else (z + step) % 8
        i = 2 * step + (h if step < 3 else 0)
        return send(half(c, h), half(c, h), s_z.at[way, i], r_z.at[way, i],
                    (4 * (zr if way == 0 else zl) + g, depth))

    def halves(way, step):
        return (0, 1) if step < 3 else (way,)

    def part(c, kind, at, start, count):
        return wfull.at[c, kind, pl.ds(pl.multiple_of(64 * at + start, 32), count)]

    def narrow(kind, way, step):
        c = (z + 8 - step) % 8 if way == 0 else (z + step) % 8
        rows_sent = part(c, kind, x, 0, 64) if step < 3 else part(c, kind, x, 32 * way, 32)
        return send(rows_sent, rows_sent, s_b.at[kind // 2, way, step], r_b.at[kind // 2, way, step],
                    (4 * (zr if way == 0 else zl) + g, depth))

    def chunk_of(i):
        return (z + 8 - i) % 8 if i < 4 else (z + i - 3) % 8

    def spread(kind, way, i):
        rows_sent = part(chunk_of(i), kind, x, 0, 64)
        return send(rows_sent, rows_sent, s_x.at[kind // 2, way, i], r_x.at[kind // 2, way, i],
                    (tm, 4 * (xr if way == 0 else xl) + yh))

    def pass_on(kind, way, i):
        rows_sent = part(chunk_of(i), kind, xl if way == 0 else xr, 32 * way, 32)
        return send(rows_sent, rows_sent, s_f.at[kind // 2, way, i], r_f.at[kind // 2, way, i],
                    (tm, 4 * (xr if way == 0 else xl) + yh))

    def relay(kind, i):
        for way in (0, 1):
            spread(kind, way, i).wait_recv()
            pass_on(kind, way, i).start()

    def advance(kind, step):
        for way in (0, 1):
            narrow(kind, way, step).wait_recv()
            if step < 3:
                narrow(kind, way, step + 1).start()
                for to in (0, 1):
                    spread(kind, to, (1 if way == 0 else 4) + step).start()
        if step == 3:
            for to in (0, 1):
                spread(kind, to, 7).start()

    def enter(kind):
        pltpu.make_async_copy(wp.at[0], part(z, kind, x, 0, 64), r_e.at[kind]).wait()
        for way in (0, 1):
            narrow(kind, way, 0).start()
        for way in (0, 1):
            spread(kind, way, 0).start()

    near, far = 2 * (g // 2), 2 - 2 * (g // 2)

    def multiply(i, first, kind, base, count):
        c = chunk_of(i)
        cols = pl.ds(pl.multiple_of(c * 256, 256), 256)
        who = pl.ds(base, count)
        product = jnp.dot(tok[who, :, cols].reshape(128 * count, 256), wfull[c, kind],
                          preferred_element_type=F32).reshape(count, 128, 256)
        acc[kind, who] = product if first else acc[kind, who] + product

    def others(i, base, count):
        lax.fori_loop(1, 3, lambda kind, t: multiply(i, i == 0, kind, base, count), None)

    def landed(kind, i):
        for way in (0, 1):
            pass_on(kind, way, i).wait_recv()

    enter(2)
    for i in range(4):
        pltpu.make_async_copy(wp.at[0], wfull.at[z, 1, pl.ds(64 * i, 64)], r_d.at[i]).wait()
    for h in (0, 1):
        for way in (0, 1):
            ring(way, 0, h).start()
    enter(0)
    for step in range(4):
        advance(2, step)
        for h in (0, 1):
            for way in (0, 1):
                if h in halves(way, step):
                    ring(way, step, h).wait_recv()
                    if step < 3 and h in halves(way, step + 1):
                        ring(way, step + 1, h).start()
        if step == 0:
            relay(2, 0)
        else:
            relay(2, step)
            relay(2, step + 3)
        advance(0, step)
        if step == 1:
            relay(0, 0)
            t_partner.wait_recv()
            landed(2, 0)
            others(0, near, 2)
        if step == 2:
            relay(0, 1)
            relay(0, 4)
            t_across.wait_recv()
            t_relay.start()
            landed(2, 1)
            others(1, near, 2)
            landed(2, 4)
            others(4, near, 2)
    relay(2, 7)
    relay(0, 2)
    relay(0, 5)
    for i in (2, 5):
        landed(2, i)
        others(i, near, 2)
    t_relay.wait_recv()
    for i in (0, 1, 4, 2, 5):
        others(i, far, 2)
    for i in (3, 6, 7):
        landed(2, i)
        others(i, 0, 4)

    for b in range(4):
        kv[2 + b, :, :256] = acc[1, b].astype(BF)
        kv[2 + b, :, 256:] = acc[2, b].astype(BF)
    kv_ahead = send(kv.at[pl.ds(4, 2)], kv.at[pl.ds(0, 2)], s_kv.at[0], r_kv.at[0], (4 * zr + g, depth))
    kv_back = send(kv.at[pl.ds(2, 2)], kv.at[pl.ds(6, 2)], s_kv.at[1], r_kv.at[1], (4 * zl + g, depth))
    kv_ahead.start()
    kv_back.start()
    for i in (3, 6, 7):
        relay(0, i)
    for i in (0, 1, 4, 2, 5, 3, 6, 7):
        landed(0, i)
        multiply(i, i == 0, 0, 0, 4)
    q[...] = acc[0].astype(BF)
    for c in m_copies:
        c.wait()
    kv_ahead.wait()
    kv_back.wait()

    def attend(b):
        row = masks[b]
        allowed = jnp.concatenate([jnp.broadcast_to(row[:, e:e + 1], (1, 128)) for e in range(5)], axis=1) > 0
        halves_out = []
        for h in range(2):
            keys = kv[pl.ds(b, 5), :, 128 * h:128 * h + 128].reshape(640, 128)
            values = kv[pl.ds(b, 5), :, 256 + 128 * h:384 + 128 * h].reshape(640, 128)
            query = q[b, :, 128 * h:128 * h + 128]
            scores = lax.dot_general(query, keys, (((1,), (1,)), ((), ())),
                                     preferred_element_type=F32) * (1.0 / math.sqrt(HD))
            scores = jnp.where(allowed, scores, -1e30)
            powers = jnp.exp(scores - jnp.max(scores, axis=-1, keepdims=True))
            weights = (powers / jnp.sum(powers, axis=-1, keepdims=True)).astype(BF)
            halves_out.append(jnp.dot(weights, values, preferred_element_type=F32).astype(BF))
        return halves_out

    def give(k):
        return send(ctx_out.at[k - 1], ctx_in.at[g], s_c.at[k - 1], r_c.at[k - 1],
                    (4 * z + (g + k) % 4, depth))

    for k in (2, 3, 1, 0):
        pieces = attend((g + k) % 4)
        for h in range(2):
            if k:
                ctx_out[k - 1, :, 128 * h:128 * h + 128] = pieces[h]
            else:
                ctx_in[g, :, 128 * h:128 * h + 128] = pieces[h]
        if k:
            give(k).start()

    for j in range(3):
        direct(j, lambda c: c.wait_send(), lambda c: None)
    t_across.wait_send()
    t_partner.wait_send()
    t_relay.wait_send()
    for way in (0, 1):
        for step in range(4):
            for h in halves(way, step):
                ring(way, step, h).wait_send()
            for kind in (0, 2):
                narrow(kind, way, step).wait_send()
        for i in range(8):
            for kind in (0, 2):
                spread(kind, way, i).wait_send()
                pass_on(kind, way, i).wait_send()
    for k in (2, 3, 1):
        give(k).wait()
    for i in range(4):
        out[:, 256 * i:256 * i + 256] = ctx_in[i]


def per_device(raw, stream, conv_w, gain, w_qkv, mask):
    vmem = pltpu.VMEM
    dma = pltpu.SemaphoreType.DMA
    context = pl.pallas_call(
        layer,
        out_shape=jax.ShapeDtypeStruct((128, 1024), BF),
        in_specs=[pl.BlockSpec(memory_space=pltpu.HBM)] * 6,
        out_specs=pl.BlockSpec(memory_space=pltpu.VMEM),
        scratch_shapes=[
            vmem((16, 8, 128), BF), vmem((128, 2048), BF), vmem((3, 128, 2048), BF), vmem((1, 2048), F32),
            vmem((16, 16, 128), F32), vmem((16, 8, 128), BF), vmem((16, 8, 128), BF),
            vmem((128, 2048), F32), vmem((4, 128, 2048), BF), vmem((4, 64, 192), BF),
            vmem((3, 64, 256), BF), vmem((8, 3, 256, 256), BF), vmem((3, 4, 128, 256), F32),
            vmem((4, 128, 256), BF), vmem((8, 128, 512), BF), vmem((4, 1, 5), jnp.int32),
            vmem((3, 128, 256), BF), vmem((4, 128, 256), BF),
            dma((6,)), dma((3,)), dma((3,)), dma((2,)), dma((2,)), dma((3,)), dma((3,)),
            dma((3, 4)), dma((4,)), dma((3,)), dma((3,)), dma((3,)), dma((3,)),
            dma((2, 7)), dma((2, 7)), dma((2, 2, 4)), dma((2, 2, 4)), dma((2, 2, 8)), dma((2, 2, 8)),
            dma((2, 2, 8)), dma((2, 2, 8)), dma((2,)), dma((2,)), dma((3,)), dma((3,)),
        ],
        compiler_params=pltpu.CompilerParams(
            collective_id=0, has_side_effects=True, vmem_limit_bytes=48 * 1024 * 1024),
    )(*[pltpu.with_memory_space_constraint(a, pltpu.HBM) for a in (
        raw, stream.reshape(128, 2048), conv_w, gain.reshape(1, 2048), w_qkv, mask.reshape(1, 5))])
    return context.reshape(16, 8, 1024)


def solution(mesh):
    in_specs = (P("tm", "depth", None), P("tm", "depth", None), P(), P(), P("tm", "depth"),
                P("depth", "tm", None))
    return jax.shard_map(per_device, mesh=mesh, in_specs=in_specs,
                         out_specs=P("tm", "depth", None), check_vma=False)
```

```python
import math

import jax
import jax.numpy as jnp
from jax import lax
from jax.experimental import pallas as pl
from jax.experimental.pallas import tpu as pltpu
from jax.sharding import PartitionSpec as P

HEADS = 8
HD = 128
BF = jnp.bfloat16
F32 = jnp.float32


def layer(raw_h, stream_h, conv_h, gain_h, w_h, mask_h, out, raw, stream, conv, gain, pad, rleft, rright,
          emb, tok, wy, wp, wfull, acc, q, kv, masks, ctx_out, ctx_in, s_in, s_w, r_w, s_raw, r_raw,
          s_m, r_m, s_d, r_d, s_e, r_e, s_t, r_t, s_z, r_z, s_b, r_b, s_x, r_x, s_f, r_f, s_l, r_l, s_kv, r_kv,
          s_c, r_c):
    tm, depth = lax.axis_index("tm"), lax.axis_index("depth")
    z, g = tm // 4, tm % 4
    x, yh = depth // 4, depth % 4
    up, down = (depth + 1) % 16, (depth + 15) % 16
    zr, zl = (z + 1) % 8, (z + 7) % 8
    xr, xl = (x + 1) % 4, (x + 3) % 4

    loads = [pltpu.make_async_copy(a, b, s_in.at[i]) for i, (a, b) in enumerate(
        ((w_h, wy.at[yh]), (raw_h, raw), (conv_h, conv), (stream_h, stream), (gain_h, gain),
         (mask_h, masks.at[g])))]
    for c in loads:
        c.start()

    def send(src, dst, s, r, to):
        return pltpu.make_async_remote_copy(
            src_ref=src, dst_ref=dst, send_sem=s, recv_sem=r, device_id=to,
            device_id_type=pl.DeviceIdType.MESH)

    barrier = pltpu.get_barrier_semaphore()

    def greet(a, b):
        pl.semaphore_signal(barrier, inc=1, device_id=(a, b), device_id_type=pl.DeviceIdType.MESH)

    for k in range(1, 4):
        greet(tm, 4 * x + (yh + k) % 4)
    greet(tm, up)
    greet(tm, down)
    greet(4 * zr + g, depth)
    greet(4 * zl + g, depth)
    for a in range(4):
        for b in range(4):
            if a or b:
                greet(4 * z + (g + a) % 4, 4 * ((x + b) % 4) + yh)
    pl.semaphore_wait(barrier, 22)

    w_copies = [send(w_h, wy.at[yh], s_w.at[k - 1], r_w.at[k - 1], (tm, 4 * x + (yh + k) % 4))
                for k in range(1, 4)]
    for c in w_copies:
        c.start()
    raw_up = send(raw_h, rleft, s_raw.at[0], r_raw.at[0], (tm, up))
    raw_down = send(raw_h, rright, s_raw.at[1], r_raw.at[1], (tm, down))
    raw_up.start()
    raw_down.start()
    m_copies = [send(mask_h, masks.at[g], s_m.at[k - 1], r_m.at[k - 1], (4 * z + (g + k) % 4, depth))
                for k in range(1, 4)]
    for c in m_copies:
        c.start()

    loads[0].wait()
    for c in w_copies:
        c.wait()
    parts = [wy[i].astype(F32) for i in range(4)]
    wp[0] = jnp.concatenate([parts[0], parts[1][:, :64]], axis=1).astype(BF)
    wp[1] = jnp.concatenate([parts[1][:, 64:], parts[2][:, :128]], axis=1).astype(BF)
    wp[2] = jnp.concatenate([parts[2][:, 128:], parts[3]], axis=1).astype(BF)
    rows = pl.ds(pl.multiple_of(g * 64, 64), 64)

    def to_all(j, k):
        pair = 3 * x + j
        return send(wp.at[j], wfull.at[z, 0, rows], s_d.at[j, k], r_d.at[g],
                    (4 * z + pair % 4, 4 * ((x + k) % 4) + yh))

    def to_one(j):
        pair = 3 * x + j
        return send(wp.at[j], wfull.at[z, pair // 4, rows], s_e.at[j], r_e.at[pair // 4],
                    (4 * z + pair % 4, 4 * g + yh))

    def keep_query(j):
        return pltpu.make_async_copy(wp.at[j], wfull.at[z, 0, rows], r_d.at[g])

    def keep_other(j):
        pair = 3 * x + j
        return pltpu.make_async_copy(wp.at[j], wfull.at[z, pair // 4, rows], r_e.at[pair // 4])

    def direct(j, act, stay):
        pair = 3 * x + j
        mine = pair % 4 == g

        @pl.when(pair < 4)
        def _():
            for k in range(1, 4):
                act(to_all(j, k))

            @pl.when(mine)
            def _():
                stay(keep_query(j))

            @pl.when(jnp.logical_not(mine))
            def _():
                act(to_all(j, 0))

        @pl.when(pair >= 4)
        def _():
            own = jnp.logical_and(mine, x == g)

            @pl.when(own)
            def _():
                stay(keep_other(j))

            @pl.when(jnp.logical_not(own))
            def _():
                act(to_one(j))

    for j in range(3):
        direct(j, lambda c: c.start(), lambda c: c.start())

    for c in loads[1:]:
        c.wait()
    raw_up.wait()
    raw_down.wait()
    pad[:, 1:9, :] = raw[...].astype(F32)
    pad[:, 0:1, :] = jnp.where(depth == 0, 0.0, rleft[:, 7:8, :].astype(F32))
    pad[:, 9:10, :] = jnp.where(depth == 15, 0.0, rright[:, 0:1, :].astype(F32))
    windows = [pad[:, j:j + 8, :].reshape(128, 128).astype(BF) for j in range(3)]
    squares = jnp.zeros((128, 1), F32)
    for n in range(4):
        cols = slice(512 * n, 512 * n + 512)
        e = stream[:, cols].astype(F32)
        for j in range(3):
            e = e + jnp.dot(windows[j], conv[j, :, cols], preferred_element_type=F32)
        emb[:, cols] = e
        squares = squares + jnp.sum(e * e, axis=-1, keepdims=True)
    inv = lax.rsqrt(squares * (1.0 / 2048) + 1e-05)
    tok[g] = (emb[...] * inv * gain[...]).astype(BF)
    partner = g + 1 - 2 * (g % 2)
    across = (g + 2) % 4
    t_across = send(tok.at[g], tok.at[g], s_t.at[0], r_t.at[0], (4 * z + across, depth))
    t_partner = send(tok.at[g], tok.at[g], s_t.at[1], r_t.at[1], (4 * z + partner, depth))
    t_relay = send(tok.at[across], tok.at[across], s_t.at[2], r_t.at[2], (4 * z + partner, depth))
    t_across.start()
    t_partner.start()

    def half(c, h):
        return wfull.at[c, 0, pl.ds(128 * h, 128)]

    def ring(way, step, h):
        c = (z + 8 - step) % 8 if way == 0 else (z + step) % 8
        i = 2 * step + (h if step < 3 else 0)
        return send(half(c, h), half(c, h), s_z.at[way, i], r_z.at[way, i],
                    (4 * (zr if way == 0 else zl) + g, depth))

    def halves(way, step):
        return (0, 1) if step < 3 else (way,)

    def quarter(c, kinds, at):
        return wfull.at[c, kinds, pl.ds(pl.multiple_of(64 * at, 64), 64)]

    both = pl.ds(1, 2)

    def narrow(way, step):
        c = (z + 8 - step) % 8 if way == 0 else (z + step) % 8
        part = quarter(c, both if step < 3 else pl.ds(1 + way, 1), x)
        return send(part, part, s_b.at[way, step], r_b.at[way, step],
                    (4 * (zr if way == 0 else zl) + g, depth))

    def chunk_of(i):
        return (z + 8 - i) % 8 if i < 4 else (z + i - 3) % 8

    def spread(way, i):
        part = quarter(chunk_of(i), both, x)
        return send(part, part, s_x.at[way, i], r_x.at[way, i], (tm, 4 * (xr if way == 0 else xl) + yh))

    def pass_on(way, i):
        part = quarter(chunk_of(i), pl.ds(1 + way, 1), xl if way == 0 else xr)
        return send(part, part, s_f.at[way, i], r_f.at[way, i], (tm, 4 * (xr if way == 0 else xl) + yh))

    def leap():
        part = quarter(chunk_of(7), both, x)
        return send(part, part, s_l.at[0], r_l.at[0], (tm, 4 * ((x + 2) % 4) + yh))

    def relay(i):
        for way in (0, 1):
            spread(way, i).wait_recv()
            pass_on(way, i).start()

    near, far = 2 * (g // 2), 2 - 2 * (g // 2)

    def multiply(i, first, kind, base, count):
        c = chunk_of(i)
        cols = pl.ds(pl.multiple_of(c * 256, 256), 256)
        who = pl.ds(base, count)
        product = jnp.dot(tok[who, :, cols].reshape(128 * count, 256), wfull[c, kind],
                          preferred_element_type=F32).reshape(count, 128, 256)
        acc[kind, who] = product if first else acc[kind, who] + product

    def others(i, base, count):
        lax.fori_loop(1, 3, lambda kind, t: multiply(i, i == 0, kind, base, count), None)

    def landed(i):
        for way in (0, 1):
            pass_on(way, i).wait_recv()

    for kind in (1, 2):
        pltpu.make_async_copy(wp.at[0], quarter(z, kind, x), r_e.at[kind]).wait()
    for way in (0, 1):
        narrow(way, 0).start()
    for way in (0, 1):
        spread(way, 0).start()
    for i in range(4):
        pltpu.make_async_copy(wp.at[0], wfull.at[z, 0, pl.ds(64 * i, 64)], r_d.at[i]).wait()
    for h in (0, 1):
        for way in (0, 1):
            ring(way, 0, h).start()
    for step in range(4):
        for way in (0, 1):
            narrow(way, step).wait_recv()
            if step < 3:
                narrow(way, step + 1).start()
                for to in (0, 1):
                    spread(to, (1 if way == 0 else 4) + step).start()
        if step == 3:
            leap().start()
            for to in (0, 1):
                spread(to, 7).start()
        for h in (0, 1):
            for way in (0, 1):
                if h in halves(way, step):
                    ring(way, step, h).wait_recv()
                    if step < 3 and h in halves(way, step + 1):
                        ring(way, step + 1, h).start()
        if step == 0:
            relay(0)
        else:
            relay(step)
            relay(step + 3)
        if step == 1:
            t_partner.wait_recv()
            landed(0)
            others(0, near, 2)
        if step == 2:
            landed(1)
            others(1, near, 2)
            landed(4)
            others(4, near, 2)
    t_across.wait_recv()
    t_relay.start()
    for i in (2, 5):
        landed(i)
        others(i, near, 2)
    t_relay.wait_recv()
    for i in (0, 1, 4, 2, 5):
        others(i, far, 2)
    for i in (3, 6):
        landed(i)
        others(i, 0, 4)
    for way in (0, 1):
        spread(way, 7).wait_recv()
    leap().wait_recv()
    others(7, 0, 4)

    for b in range(4):
        kv[2 + b, :, :256] = acc[1, b].astype(BF)
        kv[2 + b, :, 256:] = acc[2, b].astype(BF)
    kv_ahead = send(kv.at[pl.ds(4, 2)], kv.at[pl.ds(0, 2)], s_kv.at[0], r_kv.at[0], (4 * zr + g, depth))
    kv_back = send(kv.at[pl.ds(2, 2)], kv.at[pl.ds(6, 2)], s_kv.at[1], r_kv.at[1], (4 * zl + g, depth))
    kv_ahead.start()
    kv_back.start()
    for i in range(8):
        multiply(i, i == 0, 0, 0, 4)
    q[...] = acc[0].astype(BF)
    for c in m_copies:
        c.wait()
    kv_ahead.wait()
    kv_back.wait()

    def attend(b):
        row = masks[b]
        allowed = jnp.concatenate([jnp.broadcast_to(row[:, e:e + 1], (1, 128)) for e in range(5)], axis=1) > 0
        halves_out = []
        for h in range(2):
            keys = kv[pl.ds(b, 5), :, 128 * h:128 * h + 128].reshape(640, 128)
            values = kv[pl.ds(b, 5), :, 256 + 128 * h:384 + 128 * h].reshape(640, 128)
            query = q[b, :, 128 * h:128 * h + 128]
            scores = lax.dot_general(query, keys, (((1,), (1,)), ((), ())),
                                     preferred_element_type=F32) * (1.0 / math.sqrt(HD))
            scores = jnp.where(allowed, scores, -1e30)
            powers = jnp.exp(scores - jnp.max(scores, axis=-1, keepdims=True))
            weights = (powers / jnp.sum(powers, axis=-1, keepdims=True)).astype(BF)
            halves_out.append(jnp.dot(weights, values, preferred_element_type=F32).astype(BF))
        return halves_out

    def give(k):
        return send(ctx_out.at[k - 1], ctx_in.at[g], s_c.at[k - 1], r_c.at[k - 1],
                    (4 * z + (g + k) % 4, depth))

    for k in (2, 3, 1, 0):
        pieces = attend((g + k) % 4)
        for h in range(2):
            if k:
                ctx_out[k - 1, :, 128 * h:128 * h + 128] = pieces[h]
            else:
                ctx_in[g, :, 128 * h:128 * h + 128] = pieces[h]
        if k:
            give(k).start()

    for j in range(3):
        direct(j, lambda c: c.wait_send(), lambda c: None)
    t_across.wait_send()
    t_partner.wait_send()
    t_relay.wait_send()
    for way in (0, 1):
        for step in range(4):
            for h in halves(way, step):
                ring(way, step, h).wait_send()
            narrow(way, step).wait_send()
        for i in range(8):
            spread(way, i).wait_send()
            if i < 7:
                pass_on(way, i).wait_send()
    leap().wait_send()
    for k in (2, 3, 1):
        give(k).wait()
    for i in range(4):
        out[:, 256 * i:256 * i + 256] = ctx_in[i]


def per_device(raw, stream, conv_w, gain, w_qkv, mask):
    vmem = pltpu.VMEM
    dma = pltpu.SemaphoreType.DMA
    context = pl.pallas_call(
        layer,
        out_shape=jax.ShapeDtypeStruct((128, 1024), BF),
        in_specs=[pl.BlockSpec(memory_space=pltpu.HBM)] * 6,
        out_specs=pl.BlockSpec(memory_space=pltpu.VMEM),
        scratch_shapes=[
            vmem((16, 8, 128), BF), vmem((128, 2048), BF), vmem((3, 128, 2048), BF), vmem((1, 2048), F32),
            vmem((16, 16, 128), F32), vmem((16, 8, 128), BF), vmem((16, 8, 128), BF),
            vmem((128, 2048), F32), vmem((4, 128, 2048), BF), vmem((4, 64, 192), BF),
            vmem((3, 64, 256), BF), vmem((8, 3, 256, 256), BF), vmem((3, 4, 128, 256), F32),
            vmem((4, 128, 256), BF), vmem((8, 128, 512), BF), vmem((4, 1, 5), jnp.int32),
            vmem((3, 128, 256), BF), vmem((4, 128, 256), BF),
            dma((6,)), dma((3,)), dma((3,)), dma((2,)), dma((2,)), dma((3,)), dma((3,)),
            dma((3, 4)), dma((4,)), dma((3,)), dma((3,)), dma((3,)), dma((3,)),
            dma((2, 7)), dma((2, 7)), dma((2, 4)), dma((2, 4)), dma((2, 8)), dma((2, 8)),
            dma((2, 7)), dma((2, 7)), dma((1,)), dma((1,)), dma((2,)), dma((2,)), dma((3,)), dma((3,)),
        ],
        compiler_params=pltpu.CompilerParams(
            collective_id=0, has_side_effects=True, vmem_limit_bytes=48 * 1024 * 1024),
    )(*[pltpu.with_memory_space_constraint(a, pltpu.HBM) for a in (
        raw, stream.reshape(128, 2048), conv_w, gain.reshape(1, 2048), w_qkv, mask.reshape(1, 5))])
    return context.reshape(16, 8, 1024)


def solution(mesh):
    in_specs = (P("tm", "depth", None), P("tm", "depth", None), P(), P(), P("tm", "depth"),
                P("depth", "tm", None))
    return jax.shard_map(per_device, mesh=mesh, in_specs=in_specs,
                         out_specs=P("tm", "depth", None), check_vma=False)
```

```python
import math

import jax
import jax.numpy as jnp
from jax import lax
from jax.experimental import pallas as pl
from jax.experimental.pallas import tpu as pltpu
from jax.sharding import PartitionSpec as P

HEADS = 8
HD = 128
BF = jnp.bfloat16
F32 = jnp.float32


def layer(raw_h, stream_h, conv_h, gain_h, w_h, mask_h, out, raw, stream, conv, gain, pad, rleft, rright,
          emb, tok, wy, wp, wfull, acc, q, kv, masks, ctx_out, ctx_in, s_in, s_w, r_w, s_raw, r_raw,
          s_m, r_m, s_d, r_d, s_e, r_e, s_t, r_t, s_z, r_z, s_b, r_b, s_x, r_x, s_f, r_f, s_kv, r_kv,
          s_c, r_c):
    tm, depth = lax.axis_index("tm"), lax.axis_index("depth")
    z, g = tm // 4, tm % 4
    x, yh = depth // 4, depth % 4
    up, down = (depth + 1) % 16, (depth + 15) % 16
    zr, zl = (z + 1) % 8, (z + 7) % 8
    xr, xl = (x + 1) % 4, (x + 3) % 4

    loads = [pltpu.make_async_copy(a, b, s_in.at[i]) for i, (a, b) in enumerate(
        ((w_h, wy.at[yh]), (raw_h, raw), (conv_h, conv), (stream_h, stream), (gain_h, gain),
         (mask_h, masks.at[g])))]
    for c in loads:
        c.start()

    def send(src, dst, s, r, to):
        return pltpu.make_async_remote_copy(
            src_ref=src, dst_ref=dst, send_sem=s, recv_sem=r, device_id=to,
            device_id_type=pl.DeviceIdType.MESH)

    barrier = pltpu.get_barrier_semaphore()

    def greet(a, b):
        pl.semaphore_signal(barrier, inc=1, device_id=(a, b), device_id_type=pl.DeviceIdType.MESH)

    for k in range(1, 4):
        greet(tm, 4 * x + (yh + k) % 4)
    greet(tm, up)
    greet(tm, down)
    greet(4 * zr + g, depth)
    greet(4 * zl + g, depth)
    for a in range(4):
        for b in range(4):
            if a or b:
                greet(4 * z + (g + a) % 4, 4 * ((x + b) % 4) + yh)
    pl.semaphore_wait(barrier, 22)

    w_copies = [send(w_h, wy.at[yh], s_w.at[k - 1], r_w.at[k - 1], (tm, 4 * x + (yh + k) % 4))
                for k in range(1, 4)]
    for c in w_copies:
        c.start()
    raw_up = send(raw_h, rleft, s_raw.at[0], r_raw.at[0], (tm, up))
    raw_down = send(raw_h, rright, s_raw.at[1], r_raw.at[1], (tm, down))
    raw_up.start()
    raw_down.start()
    m_copies = [send(mask_h, masks.at[g], s_m.at[k - 1], r_m.at[k - 1], (4 * z + (g + k) % 4, depth))
                for k in range(1, 4)]
    for c in m_copies:
        c.start()

    loads[0].wait()
    for c in w_copies:
        c.wait()
    parts = [wy[i].astype(F32) for i in range(4)]
    wp[0] = jnp.concatenate([parts[0], parts[1][:, :64]], axis=1).astype(BF)
    wp[1] = jnp.concatenate([parts[1][:, 64:], parts[2][:, :128]], axis=1).astype(BF)
    wp[2] = jnp.concatenate([parts[2][:, 128:], parts[3]], axis=1).astype(BF)
    rows = pl.ds(pl.multiple_of(g * 64, 64), 64)

    def to_all(j, k):
        pair = 3 * x + j
        return send(wp.at[j], wfull.at[z, 0, rows], s_d.at[j, k], r_d.at[g],
                    (4 * z + pair % 4, 4 * ((x + k) % 4) + yh))

    def to_one(j):
        pair = 3 * x + j
        return send(wp.at[j], wfull.at[z, pair // 4, rows], s_e.at[j], r_e.at[pair // 4],
                    (4 * z + pair % 4, 4 * g + yh))

    def keep_query(j):
        return pltpu.make_async_copy(wp.at[j], wfull.at[z, 0, rows], r_d.at[g])

    def keep_other(j):
        pair = 3 * x + j
        return pltpu.make_async_copy(wp.at[j], wfull.at[z, pair // 4, rows], r_e.at[pair // 4])

    def direct(j, act, stay):
        pair = 3 * x + j
        mine = pair % 4 == g

        @pl.when(pair < 4)
        def _():
            for k in range(1, 4):
                act(to_all(j, k))

            @pl.when(mine)
            def _():
                stay(keep_query(j))

            @pl.when(jnp.logical_not(mine))
            def _():
                act(to_all(j, 0))

        @pl.when(pair >= 4)
        def _():
            own = jnp.logical_and(mine, x == g)

            @pl.when(own)
            def _():
                stay(keep_other(j))

            @pl.when(jnp.logical_not(own))
            def _():
                act(to_one(j))

    for j in range(3):
        direct(j, lambda c: c.start(), lambda c: c.start())

    for c in loads[1:]:
        c.wait()
    raw_up.wait()
    raw_down.wait()
    pad[:, 1:9, :] = raw[...].astype(F32)
    pad[:, 0:1, :] = jnp.where(depth == 0, 0.0, rleft[:, 7:8, :].astype(F32))
    pad[:, 9:10, :] = jnp.where(depth == 15, 0.0, rright[:, 0:1, :].astype(F32))
    windows = [pad[:, j:j + 8, :].reshape(128, 128).astype(BF) for j in range(3)]
    squares = jnp.zeros((128, 1), F32)
    for n in range(4):
        cols = slice(512 * n, 512 * n + 512)
        e = stream[:, cols].astype(F32)
        for j in range(3):
            e = e + jnp.dot(windows[j], conv[j, :, cols], preferred_element_type=F32)
        emb[:, cols] = e
        squares = squares + jnp.sum(e * e, axis=-1, keepdims=True)
    inv = lax.rsqrt(squares * (1.0 / 2048) + 1e-05)
    tok[g] = (emb[...] * inv * gain[...]).astype(BF)
    partner = g + 1 - 2 * (g % 2)
    across = (g + 2) % 4
    t_partner = send(tok.at[g], tok.at[g], s_t.at[4], r_t.at[4], (4 * z + partner, depth))

    def piece(i, i_sem, whose, to):
        rows_sent = tok.at[whose, pl.ds(64 * i, 64)]
        return send(rows_sent, rows_sent, s_t.at[i_sem + i], r_t.at[i_sem + i], (4 * z + to, depth))

    t_across = [piece(i, 0, g, across) for i in range(2)]
    t_relay = [piece(i, 2, across, partner) for i in range(2)]
    for c in t_across:
        c.start()
    t_partner.start()

    def half(c, h):
        return wfull.at[c, 0, pl.ds(128 * h, 128)]

    def ring(way, step, h):
        c = (z + 8 - step) % 8 if way == 0 else (z + step) % 8
        i = 2 * step + (h if step < 3 else 0)
        return send(half(c, h), half(c, h), s_z.at[way, i], r_z.at[way, i],
                    (4 * (zr if way == 0 else zl) + g, depth))

    def halves(way, step):
        return (0, 1) if step < 3 else (way,)

    def quarter(c, kinds, at):
        return wfull.at[c, kinds, pl.ds(pl.multiple_of(64 * at, 64), 64)]

    both = pl.ds(1, 2)

    def narrow(way, step):
        c = (z + 8 - step) % 8 if way == 0 else (z + step) % 8
        part = quarter(c, both if step < 3 else pl.ds(1 + way, 1), x)
        return send(part, part, s_b.at[way, step], r_b.at[way, step],
                    (4 * (zr if way == 0 else zl) + g, depth))

    def chunk_of(i):
        return (z + 8 - i) % 8 if i < 4 else (z + i - 3) % 8

    def spread(way, i):
        part = quarter(chunk_of(i), both, x)
        return send(part, part, s_x.at[way, i], r_x.at[way, i], (tm, 4 * (xr if way == 0 else xl) + yh))

    def pass_on(way, i):
        part = quarter(chunk_of(i), pl.ds(1 + way, 1), xl if way == 0 else xr)
        return send(part, part, s_f.at[way, i], r_f.at[way, i], (tm, 4 * (xr if way == 0 else xl) + yh))

    def relay(i):
        for way in (0, 1):
            spread(way, i).wait_recv()
            pass_on(way, i).start()

    near, far = 2 * (g // 2), 2 - 2 * (g // 2)

    def multiply(i, first, kind, base, count):
        c = chunk_of(i)
        cols = pl.ds(pl.multiple_of(c * 256, 256), 256)
        who = pl.ds(base, count)
        product = jnp.dot(tok[who, :, cols].reshape(128 * count, 256), wfull[c, kind],
                          preferred_element_type=F32).reshape(count, 128, 256)
        acc[kind, who] = product if first else acc[kind, who] + product

    def others(i, base, count):
        lax.fori_loop(1, 3, lambda kind, t: multiply(i, i == 0, kind, base, count), None)

    def landed(i):
        for way in (0, 1):
            pass_on(way, i).wait_recv()

    for kind in (1, 2):
        pltpu.make_async_copy(wp.at[0], quarter(z, kind, x), r_e.at[kind]).wait()
    for way in (0, 1):
        narrow(way, 0).start()
    for way in (0, 1):
        spread(way, 0).start()
    for i in range(4):
        pltpu.make_async_copy(wp.at[0], wfull.at[z, 0, pl.ds(64 * i, 64)], r_d.at[i]).wait()
    for h in (0, 1):
        for way in (0, 1):
            ring(way, 0, h).start()
    for step in range(4):
        for way in (0, 1):
            narrow(way, step).wait_recv()
            if step < 3:
                narrow(way, step + 1).start()
                for to in (0, 1):
                    spread(to, (1 if way == 0 else 4) + step).start()
        if step == 3:
            for to in (0, 1):
                spread(to, 7).start()
        for h in (0, 1):
            for way in (0, 1):
                if h in halves(way, step):
                    ring(way, step, h).wait_recv()
                    if step < 3 and h in halves(way, step + 1):
                        ring(way, step + 1, h).start()
        if step == 0:
            relay(0)
        else:
            relay(step)
            relay(step + 3)
        if step == 1:
            t_partner.wait_recv()
            landed(0)
            others(0, near, 2)
        if step == 2:
            landed(1)
            others(1, near, 2)
            t_across[0].wait_recv()
            t_relay[0].start()
            landed(4)
            others(4, near, 2)
            t_across[1].wait_recv()
            t_relay[1].start()
    for i in (2, 5):
        landed(i)
        others(i, near, 2)
    relay(7)
    for c in t_relay:
        c.wait_recv()
    for i in (0, 1, 4, 2, 5):
        others(i, far, 2)
    for i in (3, 6, 7):
        landed(i)
        others(i, 0, 4)

    for b in range(4):
        kv[2 + b, :, :256] = acc[1, b].astype(BF)
        kv[2 + b, :, 256:] = acc[2, b].astype(BF)
    kv_ahead = send(kv.at[pl.ds(4, 2)], kv.at[pl.ds(0, 2)], s_kv.at[0], r_kv.at[0], (4 * zr + g, depth))
    kv_back = send(kv.at[pl.ds(2, 2)], kv.at[pl.ds(6, 2)], s_kv.at[1], r_kv.at[1], (4 * zl + g, depth))
    kv_ahead.start()
    kv_back.start()
    for i in range(8):
        multiply(i, i == 0, 0, 0, 4)
    q[...] = acc[0].astype(BF)
    for c in m_copies:
        c.wait()
    kv_ahead.wait()
    kv_back.wait()

    def attend(b):
        row = masks[b]
        allowed = jnp.concatenate([jnp.broadcast_to(row[:, e:e + 1], (1, 128)) for e in range(5)], axis=1) > 0
        halves_out = []
        for h in range(2):
            keys = kv[pl.ds(b, 5), :, 128 * h:128 * h + 128].reshape(640, 128)
            values = kv[pl.ds(b, 5), :, 256 + 128 * h:384 + 128 * h].reshape(640, 128)
            query = q[b, :, 128 * h:128 * h + 128]
            scores = lax.dot_general(query, keys, (((1,), (1,)), ((), ())),
                                     preferred_element_type=F32) * (1.0 / math.sqrt(HD))
            scores = jnp.where(allowed, scores, -1e30)
            powers = jnp.exp(scores - jnp.max(scores, axis=-1, keepdims=True))
            weights = (powers / jnp.sum(powers, axis=-1, keepdims=True)).astype(BF)
            halves_out.append(jnp.dot(weights, values, preferred_element_type=F32).astype(BF))
        return halves_out

    def give(k):
        return send(ctx_out.at[k - 1], ctx_in.at[g], s_c.at[k - 1], r_c.at[k - 1],
                    (4 * z + (g + k) % 4, depth))

    for k in (2, 3, 1, 0):
        pieces = attend((g + k) % 4)
        for h in range(2):
            if k:
                ctx_out[k - 1, :, 128 * h:128 * h + 128] = pieces[h]
            else:
                ctx_in[g, :, 128 * h:128 * h + 128] = pieces[h]
        if k:
            give(k).start()

    for j in range(3):
        direct(j, lambda c: c.wait_send(), lambda c: None)
    for c in t_across + t_relay + [t_partner]:
        c.wait_send()
    for way in (0, 1):
        for step in range(4):
            for h in halves(way, step):
                ring(way, step, h).wait_send()
            narrow(way, step).wait_send()
        for i in range(8):
            spread(way, i).wait_send()
            pass_on(way, i).wait_send()
    for k in (2, 3, 1):
        give(k).wait()
    for i in range(4):
        out[:, 256 * i:256 * i + 256] = ctx_in[i]


def per_device(raw, stream, conv_w, gain, w_qkv, mask):
    vmem = pltpu.VMEM
    dma = pltpu.SemaphoreType.DMA
    context = pl.pallas_call(
        layer,
        out_shape=jax.ShapeDtypeStruct((128, 1024), BF),
        in_specs=[pl.BlockSpec(memory_space=pltpu.HBM)] * 6,
        out_specs=pl.BlockSpec(memory_space=pltpu.VMEM),
        scratch_shapes=[
            vmem((16, 8, 128), BF), vmem((128, 2048), BF), vmem((3, 128, 2048), BF), vmem((1, 2048), F32),
            vmem((16, 16, 128), F32), vmem((16, 8, 128), BF), vmem((16, 8, 128), BF),
            vmem((128, 2048), F32), vmem((4, 128, 2048), BF), vmem((4, 64, 192), BF),
            vmem((3, 64, 256), BF), vmem((8, 3, 256, 256), BF), vmem((3, 4, 128, 256), F32),
            vmem((4, 128, 256), BF), vmem((8, 128, 512), BF), vmem((4, 1, 5), jnp.int32),
            vmem((3, 128, 256), BF), vmem((4, 128, 256), BF),
            dma((6,)), dma((3,)), dma((3,)), dma((2,)), dma((2,)), dma((3,)), dma((3,)),
            dma((3, 4)), dma((4,)), dma((3,)), dma((3,)), dma((5,)), dma((5,)),
            dma((2, 7)), dma((2, 7)), dma((2, 4)), dma((2, 4)), dma((2, 8)), dma((2, 8)),
            dma((2, 8)), dma((2, 8)), dma((2,)), dma((2,)), dma((3,)), dma((3,)),
        ],
        compiler_params=pltpu.CompilerParams(
            collective_id=0, has_side_effects=True, vmem_limit_bytes=48 * 1024 * 1024),
    )(*[pltpu.with_memory_space_constraint(a, pltpu.HBM) for a in (
        raw, stream.reshape(128, 2048), conv_w, gain.reshape(1, 2048), w_qkv, mask.reshape(1, 5))])
    return context.reshape(16, 8, 1024)


def solution(mesh):
    in_specs = (P("tm", "depth", None), P("tm", "depth", None), P(), P(), P("tm", "depth"),
                P("depth", "tm", None))
    return jax.shard_map(per_device, mesh=mesh, in_specs=in_specs,
                         out_specs=P("tm", "depth", None), check_vma=False)
```

```python
import math

import jax
import jax.numpy as jnp
from jax import lax
from jax.experimental import pallas as pl
from jax.experimental.pallas import tpu as pltpu
from jax.sharding import PartitionSpec as P

HEADS = 8
HD = 128
BF = jnp.bfloat16
F32 = jnp.float32


def layer(raw_h, stream_h, conv_h, gain_h, w_h, mask_h, out, raw, stream, conv, gain, pad, rleft, rright,
          emb, tok, wy, wp, wfull, acc, q, kv, masks, ctx_out, ctx_in, s_in, s_w, r_w, s_raw, r_raw,
          s_m, r_m, s_d, r_d, s_e, r_e, s_t, r_t, s_z, r_z, s_b, r_b, s_x, r_x, s_f, r_f, s_kv, r_kv,
          s_c, r_c):
    tm, depth = lax.axis_index("tm"), lax.axis_index("depth")
    z, g = tm // 4, tm % 4
    x, yh = depth // 4, depth % 4
    up, down = (depth + 1) % 16, (depth + 15) % 16
    zr, zl = (z + 1) % 8, (z + 7) % 8
    xr, xl = (x + 1) % 4, (x + 3) % 4

    loads = [pltpu.make_async_copy(a, b, s_in.at[i]) for i, (a, b) in enumerate(
        ((w_h, wy.at[yh]), (raw_h, raw), (conv_h, conv), (stream_h, stream), (gain_h, gain),
         (mask_h, masks.at[g])))]
    for c in loads:
        c.start()

    def send(src, dst, s, r, to):
        return pltpu.make_async_remote_copy(
            src_ref=src, dst_ref=dst, send_sem=s, recv_sem=r, device_id=to,
            device_id_type=pl.DeviceIdType.MESH)

    barrier = pltpu.get_barrier_semaphore()

    def greet(a, b):
        pl.semaphore_signal(barrier, inc=1, device_id=(a, b), device_id_type=pl.DeviceIdType.MESH)

    for k in range(1, 4):
        greet(tm, 4 * x + (yh + k) % 4)
    greet(tm, up)
    greet(tm, down)
    greet(4 * zr + g, depth)
    greet(4 * zl + g, depth)
    for a in range(4):
        for b in range(4):
            if a or b:
                greet(4 * z + (g + a) % 4, 4 * ((x + b) % 4) + yh)
    pl.semaphore_wait(barrier, 22)

    w_copies = [send(w_h, wy.at[yh], s_w.at[k - 1], r_w.at[k - 1], (tm, 4 * x + (yh + k) % 4))
                for k in range(1, 4)]
    for c in w_copies:
        c.start()
    raw_up = send(raw_h, rleft, s_raw.at[0], r_raw.at[0], (tm, up))
    raw_down = send(raw_h, rright, s_raw.at[1], r_raw.at[1], (tm, down))
    raw_up.start()
    raw_down.start()
    m_copies = [send(mask_h, masks.at[g], s_m.at[k - 1], r_m.at[k - 1], (4 * z + (g + k) % 4, depth))
                for k in range(1, 4)]
    for c in m_copies:
        c.start()

    loads[0].wait()
    for c in w_copies:
        c.wait()
    parts = [wy[i].astype(F32) for i in range(4)]
    wp[0] = jnp.concatenate([parts[0], parts[1][:, :64]], axis=1).astype(BF)
    wp[1] = jnp.concatenate([parts[1][:, 64:], parts[2][:, :128]], axis=1).astype(BF)
    wp[2] = jnp.concatenate([parts[2][:, 128:], parts[3]], axis=1).astype(BF)
    rows = pl.ds(pl.multiple_of(g * 64, 64), 64)

    def to_all(j, k):
        pair = 3 * x + j
        return send(wp.at[j], wfull.at[z, 0, rows], s_d.at[j, k], r_d.at[g],
                    (4 * z + pair % 4, 4 * ((x + k) % 4) + yh))

    def to_one(j):
        pair = 3 * x + j
        return send(wp.at[j], wfull.at[z, pair // 4, rows], s_e.at[j], r_e.at[pair // 4],
                    (4 * z + pair % 4, 4 * g + yh))

    def keep_query(j):
        return pltpu.make_async_copy(wp.at[j], wfull.at[z, 0, rows], r_d.at[g])

    def keep_other(j):
        pair = 3 * x + j
        return pltpu.make_async_copy(wp.at[j], wfull.at[z, pair // 4, rows], r_e.at[pair // 4])

    def direct(j, act, stay):
        pair = 3 * x + j
        mine = pair % 4 == g

        @pl.when(pair < 4)
        def _():
            for k in range(1, 4):
                act(to_all(j, k))

            @pl.when(mine)
            def _():
                stay(keep_query(j))

            @pl.when(jnp.logical_not(mine))
            def _():
                act(to_all(j, 0))

        @pl.when(pair >= 4)
        def _():
            own = jnp.logical_and(mine, x == g)

            @pl.when(own)
            def _():
                stay(keep_other(j))

            @pl.when(jnp.logical_not(own))
            def _():
                act(to_one(j))

    for j in range(3):
        direct(j, lambda c: c.start(), lambda c: c.start())

    for c in loads[1:]:
        c.wait()
    raw_up.wait()
    raw_down.wait()
    pad[:, 1:9, :] = raw[...].astype(F32)
    pad[:, 0:1, :] = jnp.where(depth == 0, 0.0, rleft[:, 7:8, :].astype(F32))
    pad[:, 9:10, :] = jnp.where(depth == 15, 0.0, rright[:, 0:1, :].astype(F32))
    windows = [pad[:, j:j + 8, :].reshape(128, 128).astype(BF) for j in range(3)]
    squares = jnp.zeros((128, 1), F32)
    for n in range(4):
        cols = slice(512 * n, 512 * n + 512)
        e = stream[:, cols].astype(F32)
        for j in range(3):
            e = e + jnp.dot(windows[j], conv[j, :, cols], preferred_element_type=F32)
        emb[:, cols] = e
        squares = squares + jnp.sum(e * e, axis=-1, keepdims=True)
    inv = lax.rsqrt(squares * (1.0 / 2048) + 1e-05)
    tok[g] = (emb[...] * inv * gain[...]).astype(BF)
    partner = g + 1 - 2 * (g % 2)
    across = (g + 2) % 4
    t_across = send(tok.at[g], tok.at[g], s_t.at[0], r_t.at[0], (4 * z + across, depth))
    t_partner = send(tok.at[g], tok.at[g], s_t.at[1], r_t.at[1], (4 * z + partner, depth))
    t_relay = send(tok.at[across], tok.at[across], s_t.at[2], r_t.at[2], (4 * z + partner, depth))
    t_across.start()
    t_partner.start()

    def half(c, h):
        return wfull.at[c, 0, pl.ds(128 * h, 128)]

    def ring(way, step, h):
        c = (z + 8 - step) % 8 if way == 0 else (z + step) % 8
        i = 2 * step + (h if step < 3 else 0)
        return send(half(c, h), half(c, h), s_z.at[way, i], r_z.at[way, i],
                    (4 * (zr if way == 0 else zl) + g, depth))

    def halves(way, step):
        return (0, 1) if step < 3 else (way,)

    def quarter(c, kinds, at):
        return wfull.at[c, kinds, pl.ds(pl.multiple_of(64 * at, 64), 64)]

    both = pl.ds(1, 2)

    def narrow(way, step):
        c = (z + 8 - step) % 8 if way == 0 else (z + step) % 8
        part = quarter(c, both if step < 3 else pl.ds(1 + way, 1), x)
        return send(part, part, s_b.at[way, step], r_b.at[way, step],
                    (4 * (zr if way == 0 else zl) + g, depth))

    def chunk_of(i):
        return (z + 8 - i) % 8 if i < 4 else (z + i - 3) % 8

    def spread(way, i):
        part = quarter(chunk_of(i), both, x)
        return send(part, part, s_x.at[way, i], r_x.at[way, i], (tm, 4 * (xr if way == 0 else xl) + yh))

    def pass_on(way, i):
        part = quarter(chunk_of(i), pl.ds(1 + way, 1), xl if way == 0 else xr)
        return send(part, part, s_f.at[way, i], r_f.at[way, i], (tm, 4 * (xr if way == 0 else xl) + yh))

    def relay(i):
        for way in (0, 1):
            spread(way, i).wait_recv()
            pass_on(way, i).start()

    near, far = 2 * (g // 2), 2 - 2 * (g // 2)

    def multiply(i, first, kind, base, count):
        c = chunk_of(i)
        cols = pl.ds(pl.multiple_of(c * 256, 256), 256)
        who = pl.ds(base, count)
        product = jnp.dot(tok[who, :, cols].reshape(128 * count, 256), wfull[c, kind],
                          preferred_element_type=F32).reshape(count, 128, 256)
        acc[kind, who] = product if first else acc[kind, who] + product

    def others(i, base, count):
        for kind in (1, 2):
            multiply(i, i == 0, kind, base, count)

    def landed(i):
        for way in (0, 1):
            pass_on(way, i).wait_recv()

    for kind in (1, 2):
        pltpu.make_async_copy(wp.at[0], quarter(z, kind, x), r_e.at[kind]).wait()
    for way in (0, 1):
        narrow(way, 0).start()
    for way in (0, 1):
        spread(way, 0).start()
    for i in range(4):
        pltpu.make_async_copy(wp.at[0], wfull.at[z, 0, pl.ds(64 * i, 64)], r_d.at[i]).wait()
    for h in (0, 1):
        for way in (0, 1):
            ring(way, 0, h).start()
    for step in range(4):
        for way in (0, 1):
            narrow(way, step).wait_recv()
            if step < 3:
                narrow(way, step + 1).start()
                for to in (0, 1):
                    spread(to, (1 if way == 0 else 4) + step).start()
        if step == 3:
            for to in (0, 1):
                spread(to, 7).start()
        for h in (0, 1):
            for way in (0, 1):
                if h in halves(way, step):
                    ring(way, step, h).wait_recv()
                    if step < 3 and h in halves(way, step + 1):
                        ring(way, step + 1, h).start()
        if step == 0:
            relay(0)
        else:
            relay(step)
            relay(step + 3)
        if step == 1:
            t_partner.wait_recv()
            landed(0)
            others(0, near, 2)
        if step == 2:
            t_across.wait_recv()
            t_relay.start()
            landed(1)
            others(1, near, 2)
            landed(4)
            others(4, near, 2)
    for i in (2, 5):
        landed(i)
        others(i, near, 2)
    relay(7)
    t_relay.wait_recv()
    for i in (0, 1, 4, 2, 5):
        others(i, far, 2)
    for i in (3, 6, 7):
        landed(i)
        others(i, 0, 4)

    for b in range(4):
        kv[2 + b, :, :256] = acc[1, b].astype(BF)
        kv[2 + b, :, 256:] = acc[2, b].astype(BF)
    kv_ahead = send(kv.at[pl.ds(4, 2)], kv.at[pl.ds(0, 2)], s_kv.at[0], r_kv.at[0], (4 * zr + g, depth))
    kv_back = send(kv.at[pl.ds(2, 2)], kv.at[pl.ds(6, 2)], s_kv.at[1], r_kv.at[1], (4 * zl + g, depth))
    kv_ahead.start()
    kv_back.start()
    for i in range(8):
        multiply(i, i == 0, 0, 0, 4)
    q[...] = acc[0].astype(BF)
    for c in m_copies:
        c.wait()
    kv_ahead.wait()
    kv_back.wait()

    def attend(b):
        row = masks[b]
        allowed = jnp.concatenate([jnp.broadcast_to(row[:, e:e + 1], (1, 128)) for e in range(5)], axis=1) > 0
        halves_out = []
        for h in range(2):
            keys = kv[pl.ds(b, 5), :, 128 * h:128 * h + 128].reshape(640, 128)
            values = kv[pl.ds(b, 5), :, 256 + 128 * h:384 + 128 * h].reshape(640, 128)
            query = q[b, :, 128 * h:128 * h + 128]
            scores = lax.dot_general(query, keys, (((1,), (1,)), ((), ())),
                                     preferred_element_type=F32) * (1.0 / math.sqrt(HD))
            scores = jnp.where(allowed, scores, -1e30)
            powers = jnp.exp(scores - jnp.max(scores, axis=-1, keepdims=True))
            weights = (powers / jnp.sum(powers, axis=-1, keepdims=True)).astype(BF)
            halves_out.append(jnp.dot(weights, values, preferred_element_type=F32).astype(BF))
        return halves_out

    def give(k):
        return send(ctx_out.at[k - 1], ctx_in.at[g], s_c.at[k - 1], r_c.at[k - 1],
                    (4 * z + (g + k) % 4, depth))

    for k in (2, 3, 1, 0):
        pieces = attend((g + k) % 4)
        for h in range(2):
            if k:
                ctx_out[k - 1, :, 128 * h:128 * h + 128] = pieces[h]
            else:
                ctx_in[g, :, 128 * h:128 * h + 128] = pieces[h]
        if k:
            give(k).start()

    for j in range(3):
        direct(j, lambda c: c.wait_send(), lambda c: None)
    t_across.wait_send()
    t_partner.wait_send()
    t_relay.wait_send()
    for way in (0, 1):
        for step in range(4):
            for h in halves(way, step):
                ring(way, step, h).wait_send()
            narrow(way, step).wait_send()
        for i in range(8):
            spread(way, i).wait_send()
            pass_on(way, i).wait_send()
    for k in (2, 3, 1):
        give(k).wait()
    for i in range(4):
        out[:, 256 * i:256 * i + 256] = ctx_in[i]


def per_device(raw, stream, conv_w, gain, w_qkv, mask):
    vmem = pltpu.VMEM
    dma = pltpu.SemaphoreType.DMA
    context = pl.pallas_call(
        layer,
        out_shape=jax.ShapeDtypeStruct((128, 1024), BF),
        in_specs=[pl.BlockSpec(memory_space=pltpu.HBM)] * 6,
        out_specs=pl.BlockSpec(memory_space=pltpu.VMEM),
        scratch_shapes=[
            vmem((16, 8, 128), BF), vmem((128, 2048), BF), vmem((3, 128, 2048), BF), vmem((1, 2048), F32),
            vmem((16, 16, 128), F32), vmem((16, 8, 128), BF), vmem((16, 8, 128), BF),
            vmem((128, 2048), F32), vmem((4, 128, 2048), BF), vmem((4, 64, 192), BF),
            vmem((3, 64, 256), BF), vmem((8, 3, 256, 256), BF), vmem((3, 4, 128, 256), F32),
            vmem((4, 128, 256), BF), vmem((8, 128, 512), BF), vmem((4, 1, 5), jnp.int32),
            vmem((3, 128, 256), BF), vmem((4, 128, 256), BF),
            dma((6,)), dma((3,)), dma((3,)), dma((2,)), dma((2,)), dma((3,)), dma((3,)),
            dma((3, 4)), dma((4,)), dma((3,)), dma((3,)), dma((3,)), dma((3,)),
            dma((2, 7)), dma((2, 7)), dma((2, 4)), dma((2, 4)), dma((2, 8)), dma((2, 8)),
            dma((2, 8)), dma((2, 8)), dma((2,)), dma((2,)), dma((3,)), dma((3,)),
        ],
        compiler_params=pltpu.CompilerParams(
            collective_id=0, has_side_effects=True, vmem_limit_bytes=48 * 1024 * 1024),
    )(*[pltpu.with_memory_space_constraint(a, pltpu.HBM) for a in (
        raw, stream.reshape(128, 2048), conv_w, gain.reshape(1, 2048), w_qkv, mask.reshape(1, 5))])
    return context.reshape(16, 8, 1024)


def solution(mesh):
    in_specs = (P("tm", "depth", None), P("tm", "depth", None), P(), P(), P("tm", "depth"),
                P("depth", "tm", None))
    return jax.shard_map(per_device, mesh=mesh, in_specs=in_specs,
                         out_specs=P("tm", "depth", None), check_vma=False)
```
